512 devices in a mesh: dp: 32 (over y, x, core), mp: 16 (over z).
Axes of the slice: x: 4, y: 4, z: 16, core: 2. Of those that a mesh axis runs over, the one named last changes fastest.
Arguments:
- tokens: bfloat16 [32768, 8192], P('dp', 'mp'), may hold values from -6 to 6
- value_weight: bfloat16 [8192, 1024], P('mp'), may hold values from -0.0625 to 0.0625
- down_panels: bfloat16 [256, 8192, 64], P('dp', 'mp'), may hold values from -0.0625 to 0.0625
- up_panels: bfloat16 [256, 64, 1024], P('dp'), may hold values from -0.75 to 0.75
- cotangent: bfloat16 [32768, 1024], P(('dp', 'mp')), may hold values from -6 to 6
- block_adapter: int32 [256], replicated, may hold values from 0 to 255, as said below
- adapter_slot: int32 [256], replicated, may hold values from 0 to 255, as said below
Outputs:
- projected: bfloat16 [32768, 1024], P(('dp', 'mp'))
- grad_tokens: bfloat16 [32768, 8192], P('dp', 'mp')
- grad_down: bfloat16 [256, 8192, 64], P('dp', 'mp')
- grad_up: bfloat16 [256, 64, 1024], P('dp')
The draws below stay inside these ranges and needn't reach their ends.
Inputs may be any that keep to these rules, and one draw needn't show every extreme that they name: `block_adapter`: the 8 blocks of one index of dp name adapters stored on 8 different owners, the owner of slot s being s // 8. `adapter_slot`: A permutation of the adapters.
All inputs are finite; a program needn't handle non-finite values.
Results may differ from the reference program's by a relative error of at most 0.005.
Values may be sent and summed in bfloat16 or wider, within the bound.
A program may use at most 128 MiB of HBM per device.

```python
import jax
import jax.numpy as jnp
from jax import lax

D = 8192
KV = 1024
RANK = 64
BLOCK_ROWS = 128
ADP_DEV = 8
ADAPTERS = 256
TOKENS = 32768
BLOCKS = 8


def layout_draw(key):
    owners = ADAPTERS // ADP_DEV
    slot = jax.random.permutation(jax.random.fold_in(key, 11), ADAPTERS).astype(jnp.int32)
    stored = jnp.argsort(slot, stable=True).astype(jnp.int32)
    heat = jax.random.randint(jax.random.fold_in(key, 12), (owners,), 0, 4) * 4096
    noise = jax.random.randint(jax.random.fold_in(key, 13), (owners, owners), 0, 8192)
    score = (heat[None, :] + noise) * owners + jnp.arange(owners, dtype=jnp.int32)[None, :]
    unused, chosen = lax.top_k(score, BLOCKS)
    local = jax.random.randint(jax.random.fold_in(key, 14), (owners, BLOCKS), 0, ADP_DEV)
    picked = stored[(chosen * ADP_DEV + local).reshape(-1)]
    return (slot, picked.astype(jnp.int32))


def draw_block_adapter(key, part):
    return layout_draw(key)[1]


def draw_adapter_slot(key, part):
    return layout_draw(key)[0]


def shard_levels(own_key, dims, shards, smallest, top_value):
    def one(dim, shards_of):
        heights = jax.random.uniform(jax.random.fold_in(jax.random.fold_in(own_key, 6), dim), (shards_of,), jnp.float32, smallest / len(shards), top_value / len(shards))
        return jnp.repeat(jnp.exp(heights), dims[dim] // shards_of).reshape((-1,) + (1,) * (len(dims) - dim - 1))

    loudness = one(*shards[0])
    for cut in shards[1:]:
        loudness = loudness * one(*cut)
    return loudness


def scatter_about(key, extent, width, bound, split=(), kind=jnp.bfloat16):
    factor_of = shard_levels(key, extent, split, -0.22, 0.18) if split else 1.0
    drawn = jax.random.normal(key, extent, jnp.float32) * width * factor_of
    return jnp.minimum(jnp.maximum(drawn, -bound), bound).astype(kind)


def setup_inputs(seed: int = 0) -> dict:
    arg_keys = jax.random.split(jax.random.key(seed), 8)
    return {
        "tokens": scatter_about(arg_keys[0], (TOKENS, D), 1.0, 6.0, ((0, 32), (1, 16))),
        "value_weight": scatter_about(arg_keys[1], (D, KV), D ** -0.5, 0.0625, ((0, 16),)),
        "down_panels": scatter_about(arg_keys[2], (ADAPTERS, D, RANK), D ** -0.5, 0.0625, ((0, 32), (1, 16))),
        "up_panels": scatter_about(arg_keys[3], (ADAPTERS, RANK, KV), RANK ** -0.5, 0.75, ((0, 32),)),
        "cotangent": scatter_about(arg_keys[4], (TOKENS, KV), 1.0, 6.0, ((0, 512),)),
        "block_adapter": draw_block_adapter(jax.random.fold_in(arg_keys[7], 71), 0),
        "adapter_slot": draw_adapter_slot(jax.random.fold_in(arg_keys[7], 71), 0),
    }


def reference(tokens, value_weight, down_panels, up_panels, cotangent, block_adapter, adapter_slot):
    blocks_all = block_adapter.shape[0]
    slots = adapter_slot[block_adapter].astype(jnp.int32)
    token_blocks = tokens.reshape(blocks_all, BLOCK_ROWS, D)
    cot_blocks = cotangent.reshape(blocks_all, BLOCK_ROWS, KV)

    def step(carry, inputs):
        acc_down, acc_up = carry
        rows_x, rows_g, slot = inputs
        panel_a = lax.dynamic_index_in_dim(down_panels, slot, 0, keepdims=False)
        panel_b = lax.dynamic_index_in_dim(up_panels, slot, 0, keepdims=False)
        base = jnp.dot(rows_x, value_weight, preferred_element_type=jnp.float32)
        down = jnp.dot(rows_x, panel_a, preferred_element_type=jnp.float32).astype(jnp.bfloat16)
        out = (base + jnp.dot(down, panel_b, preferred_element_type=jnp.float32)).astype(jnp.bfloat16)
        back = jnp.dot(rows_g, panel_b.T, preferred_element_type=jnp.float32).astype(jnp.bfloat16)
        grad_in = jnp.dot(rows_g, value_weight.T, preferred_element_type=jnp.float32)
        grad_in = (grad_in + jnp.dot(back, panel_a.T, preferred_element_type=jnp.float32)).astype(jnp.bfloat16)
        term_a = jnp.dot(rows_x.T, back, preferred_element_type=jnp.float32)
        term_b = jnp.dot(down.T, rows_g, preferred_element_type=jnp.float32)
        acc_down = acc_down.at[slot].add(term_a)
        acc_up = acc_up.at[slot].add(term_b)
        return (acc_down, acc_up), (out, grad_in)

    init = (jnp.zeros(down_panels.shape, jnp.float32), jnp.zeros(up_panels.shape, jnp.float32))
    (acc_down, acc_up), (outs, grads) = lax.scan(step, init, (token_blocks, cot_blocks, slots))
    projected = outs.reshape(blocks_all * BLOCK_ROWS, KV)
    grad_tokens = grads.reshape(blocks_all * BLOCK_ROWS, D)
    return projected, grad_tokens, acc_down.astype(jnp.bfloat16), acc_up.astype(jnp.bfloat16)
```

```python
import jax
import jax.numpy as jnp
from jax import lax
from jax.sharding import PartitionSpec as P

RANK = 64
BLOCK_ROWS = 128


def per_device(
    tokens, value_weight, down_panels, up_panels, cotangent, block_adapter, adapter_slot
):
    n_owners = lax.axis_size("dp")
    myself = lax.axis_index("dp")
    n_split = lax.axis_size("mp")
    my_part = lax.axis_index("mp")
    rows, width_dev = tokens.shape
    own_rows, kv_full = cotangent.shape
    kv_part = kv_full // n_split
    stored = down_panels.shape[0]
    blocks = rows // BLOCK_ROWS
    highest = lax.Precision.HIGHEST
    hits = block_adapter[:, None] == jnp.arange(adapter_slot.shape[0], dtype=jnp.int32)[None, :]
    slots_all = jnp.sum(jnp.where(hits, adapter_slot[None, :], 0), axis=1)
    owner_all = (slots_all // stored).reshape(n_owners, blocks)
    local_all = (slots_all % stored).reshape(n_owners, blocks)
    mine = owner_all == myself
    wanted = jnp.sum(jnp.where(mine, local_all, 0), axis=1)
    served = jnp.any(mine, axis=1)
    pick_mask = (wanted[:, None] == jnp.arange(stored, dtype=jnp.int32)[None, :]) & served[:, None]
    my_owner = lax.dynamic_index_in_dim(owner_all, myself, 0, keepdims=False)
    select_mask = my_owner[:, None] == jnp.arange(n_owners, dtype=jnp.int32)[None, :]
    select_f32 = select_mask.astype(jnp.float32)

    send_a = jnp.take(down_panels, wanted, axis=0)
    up_cols = lax.dynamic_slice_in_dim(up_panels, my_part * kv_part, kv_part, 2)
    send_b = jnp.take(up_cols, wanted, axis=0)
    got_a = lax.all_to_all(send_a, "dp", split_axis=0, concat_axis=0, tiled=True)
    got_b = lax.all_to_all(send_b, "dp", split_axis=0, concat_axis=0, tiled=True)
    panel_a = jnp.take(got_a, my_owner, axis=0)
    panel_b_cols = jnp.take(got_b, my_owner, axis=0)

    first_row = my_part * own_rows
    part_block = (jnp.arange(n_split, dtype=jnp.int32) * own_rows) // BLOCK_ROWS
    to_parts = jnp.take(panel_b_cols, part_block, axis=0)
    from_parts = lax.all_to_all(to_parts, "mp", split_axis=0, concat_axis=0, tiled=True)
    my_up = from_parts.transpose(1, 0, 2).reshape(RANK, kv_full)

    token_blocks = tokens.reshape(blocks, BLOCK_ROWS, width_dev)
    partial_value = jnp.dot(tokens, value_weight, preferred_element_type=jnp.float32)
    base = lax.psum_scatter(partial_value, "mp", scatter_dimension=0, tiled=True)
    down_part = jnp.einsum(
        "bnd,bdk->bnk", token_blocks, panel_a, preferred_element_type=jnp.float32
    )
    down = lax.psum(down_part, "mp").astype(jnp.bfloat16)
    my_down = lax.dynamic_slice_in_dim(down.reshape(rows, RANK), first_row, own_rows, 0)
    lifted = jnp.dot(my_down, my_up, preferred_element_type=jnp.float32)
    projected = (base + lifted).astype(jnp.bfloat16)

    my_back = jnp.einsum(
        "nc,kc->nk", cotangent, my_up, preferred_element_type=jnp.float32
    ).astype(jnp.bfloat16)
    back = lax.all_gather(my_back, "mp", axis=0, tiled=True).reshape(blocks, BLOCK_ROWS, RANK)

    cot_all = lax.all_gather(cotangent, "mp", axis=0, tiled=True)
    grad_base = jnp.einsum("nc,dc->nd", cot_all, value_weight, preferred_element_type=jnp.float32)
    through = jnp.einsum("bnk,bdk->bnd", back, panel_a, preferred_element_type=jnp.float32)
    grad_tokens = (grad_base + through.reshape(rows, width_dev)).astype(jnp.bfloat16)

    block_grad_a = jnp.einsum(
        "bnd,bnk->bdk", token_blocks, back, preferred_element_type=jnp.float32
    ).astype(jnp.bfloat16)
    cot_blocks = cot_all.reshape(blocks, BLOCK_ROWS, kv_full)
    cot_share = lax.dynamic_slice_in_dim(cot_blocks, my_part * kv_part, kv_part, 2)
    block_grad_b = jnp.einsum(
        "bnk,bnc->bkc", down.reshape(blocks, BLOCK_ROWS, RANK), cot_share,
        preferred_element_type=jnp.float32,
    )
    send_ga = jnp.einsum(
        "bo,bdk->odk", select_mask.astype(jnp.bfloat16), block_grad_a,
        preferred_element_type=jnp.float32,
    ).astype(jnp.bfloat16)
    send_gb = jnp.einsum("bo,bkc->okc", select_f32, block_grad_b, precision=highest)
    recv_ga = lax.all_to_all(send_ga, "dp", split_axis=0, concat_axis=0, tiled=True)
    recv_gb = lax.all_to_all(send_gb, "dp", split_axis=0, concat_axis=0, tiled=True)
    pick_f32 = pick_mask.astype(jnp.float32)
    grad_down = jnp.einsum(
        "ra,rdk->adk", pick_mask.astype(jnp.bfloat16), recv_ga, preferred_element_type=jnp.float32
    ).astype(jnp.bfloat16)
    grad_share = jnp.einsum("ra,rkc->akc", pick_f32, recv_gb, precision=highest).astype(
        jnp.bfloat16
    )
    grad_up = lax.all_gather(grad_share, "mp", axis=2, tiled=True)
    return (projected, grad_tokens, grad_down, grad_up)


def solution(mesh):
    placed = (
        P("dp", "mp"),
        P("mp", None),
        P("dp", "mp", None),
        P("dp", None, None),
        P(("dp", "mp"), None),
        P(),
        P(),
    )
    return jax.shard_map(
        per_device,
        mesh=mesh,
        in_specs=placed,
        out_specs=(P(("dp", "mp"), None), P("dp", "mp"), P("dp", "mp", None), P("dp", None, None)),
        check_vma=False,
    )
```

```python
import jax
import jax.numpy as jnp
from jax import lax
from jax.sharding import PartitionSpec as P

RANK = 64
BLOCK_ROWS = 128


def per_device(
    tokens, value_weight, down_panels, up_panels, cotangent, block_adapter, adapter_slot
):
    n_owners = lax.axis_size("dp")
    myself = lax.axis_index("dp")
    n_split = lax.axis_size("mp")
    my_part = lax.axis_index("mp")
    rows, width_dev = tokens.shape
    own_rows, kv_full = cotangent.shape
    kv_part = kv_full // n_split
    stored = down_panels.shape[0]
    blocks = rows // BLOCK_ROWS
    hits = block_adapter[:, None] == jnp.arange(adapter_slot.shape[0], dtype=jnp.int32)[None, :]
    slots_all = jnp.sum(jnp.where(hits, adapter_slot[None, :], 0), axis=1)
    owner_all = (slots_all // stored).reshape(n_owners, blocks)
    local_all = (slots_all % stored).reshape(n_owners, blocks)
    mine = owner_all == myself
    wanted = jnp.sum(jnp.where(mine, local_all, 0), axis=1)
    served = jnp.any(mine, axis=1)
    pick_mask = (wanted[:, None] == jnp.arange(stored, dtype=jnp.int32)[None, :]) & served[:, None]
    my_owner = lax.dynamic_index_in_dim(owner_all, myself, 0, keepdims=False)
    select_mask = my_owner[:, None] == jnp.arange(n_owners, dtype=jnp.int32)[None, :]

    up_cols = lax.dynamic_slice_in_dim(up_panels, my_part * kv_part, kv_part, 2)
    both = jnp.concatenate([down_panels, up_cols], axis=1)
    got = lax.all_to_all(jnp.take(both, wanted, axis=0), "dp", split_axis=0, concat_axis=0, tiled=True)
    mine_got = jnp.take(got, my_owner, axis=0)
    panel_a = mine_got[:, :width_dev]
    panel_b_cols = mine_got[:, width_dev:]
    cot_all = lax.all_gather(cotangent, "mp", axis=0, tiled=True)
    panel_b = lax.all_gather(panel_b_cols, "mp", axis=2, tiled=True)

    token_blocks = tokens.reshape(blocks, BLOCK_ROWS, width_dev)
    partial_value = jnp.dot(tokens, value_weight, preferred_element_type=jnp.float32)
    base = lax.psum_scatter(partial_value, "mp", scatter_dimension=0, tiled=True)
    down_part = jnp.einsum(
        "bnd,bdk->bnk", token_blocks, panel_a, preferred_element_type=jnp.float32
    )
    first_row = my_part * own_rows
    my_down = lax.psum_scatter(
        down_part.reshape(rows, RANK), "mp", scatter_dimension=0, tiled=True
    ).astype(jnp.bfloat16)
    down = lax.all_gather(my_down, "mp", axis=0, tiled=True)

    cot_blocks = cot_all.reshape(blocks, BLOCK_ROWS, kv_full)
    back = jnp.einsum(
        "bnc,bkc->bnk", cot_blocks, panel_b, preferred_element_type=jnp.float32
    ).astype(jnp.bfloat16)
    block_grad_a = jnp.einsum(
        "bnd,bnk->bdk", token_blocks, back, preferred_element_type=jnp.float32
    ).astype(jnp.bfloat16)
    cot_share = lax.dynamic_slice_in_dim(cot_blocks, my_part * kv_part, kv_part, 2)
    block_grad_b = jnp.einsum(
        "bnk,bnc->bkc", down.reshape(blocks, BLOCK_ROWS, RANK), cot_share,
        preferred_element_type=jnp.float32,
    ).astype(jnp.bfloat16)
    grads = jnp.concatenate([block_grad_a, block_grad_b], axis=1)
    send_g = jnp.einsum(
        "bo,bdk->odk", select_mask.astype(jnp.bfloat16), grads, preferred_element_type=jnp.float32
    ).astype(jnp.bfloat16)
    recv_g = lax.all_to_all(send_g, "dp", split_axis=0, concat_axis=0, tiled=True)
    grad_both = jnp.einsum(
        "ra,rdk->adk", pick_mask.astype(jnp.bfloat16), recv_g, preferred_element_type=jnp.float32
    ).astype(jnp.bfloat16)
    grad_down = grad_both[:, :width_dev]
    grad_up = lax.all_gather(grad_both[:, width_dev:], "mp", axis=2, tiled=True)

    my_up = lax.dynamic_index_in_dim(panel_b, first_row // BLOCK_ROWS, 0, keepdims=False)
    lifted = jnp.dot(my_down, my_up, preferred_element_type=jnp.float32)
    projected = (base + lifted).astype(jnp.bfloat16)

    grad_base = jnp.einsum("nc,dc->nd", cot_all, value_weight, preferred_element_type=jnp.float32)
    through = jnp.einsum("bnk,bdk->bnd", back, panel_a, preferred_element_type=jnp.float32)
    grad_tokens = (grad_base + through.reshape(rows, width_dev)).astype(jnp.bfloat16)
    return (projected, grad_tokens, grad_down, grad_up)


def solution(mesh):
    placed = (
        P("dp", "mp"),
        P("mp", None),
        P("dp", "mp", None),
        P("dp", None, None),
        P(("dp", "mp"), None),
        P(),
        P(),
    )
    return jax.shard_map(
        per_device,
        mesh=mesh,
        in_specs=placed,
        out_specs=(P(("dp", "mp"), None), P("dp", "mp"), P("dp", "mp", None), P("dp", None, None)),
        check_vma=False,
    )
```

```python
import functools

import jax
import jax.numpy as jnp
from jax import lax
from jax.experimental import pallas as pl
from jax.experimental.pallas import tpu as pltpu
from jax.sharding import PartitionSpec as P

RANK = 64
BLOCK_ROWS = 128


def _exchange_kernel(n, spread, *refs):
    k = len(spread)
    ins, outs = refs[:k], refs[k:2 * k]
    send_sems, recv_sems, local_sem = refs[2 * k:]
    me = lax.axis_index("mp")
    row = lax.axis_index("dp")
    barrier = pltpu.get_barrier_semaphore()
    for d in range(1, n):
        pl.semaphore_signal(
            barrier, inc=1, device_id=(row, lax.rem(me + d, n)),
            device_id_type=pl.DeviceIdType.MESH,
        )
    pl.semaphore_wait(barrier, n - 1)
    copies = []
    for a in range(k):
        for d in range(1, n):
            tgt = lax.rem(me + d, n)
            src = ins[a].at[0] if spread[a] else ins[a].at[tgt]
            copy = pltpu.make_async_remote_copy(
                src_ref=src,
                dst_ref=outs[a].at[me],
                send_sem=send_sems.at[a, d],
                recv_sem=recv_sems.at[a, d],
                device_id=(row, tgt),
                device_id_type=pl.DeviceIdType.MESH,
            )
            copy.start()
            copies.append((a, d, copy))
    for a in range(k):
        src = ins[a].at[0] if spread[a] else ins[a].at[me]
        local = pltpu.make_async_copy(src, outs[a].at[me], local_sem.at[a])
        local.start()
        local.wait()
    for a, d, copy in copies:
        copy.wait_send()
        origin = lax.rem(me + n - d, n)
        pltpu.make_async_remote_copy(
            src_ref=outs[a].at[origin],
            dst_ref=outs[a].at[origin],
            send_sem=send_sems.at[a, d],
            recv_sem=recv_sems.at[a, d],
            device_id=(row, origin),
            device_id_type=pl.DeviceIdType.MESH,
        ).wait_recv()


def mp_exchange(arrays, spread, n, tag):
    outs = tuple(
        jax.ShapeDtypeStruct((n,) + x.shape[1:], x.dtype) for x in arrays
    )
    moved = sum(x.size * x.dtype.itemsize for x in outs)
    vmem = pl.BlockSpec(memory_space=pltpu.VMEM)
    return pl.pallas_call(
        functools.partial(_exchange_kernel, n, tuple(spread)),
        out_shape=outs,
        in_specs=[vmem] * len(arrays),
        out_specs=tuple([vmem] * len(arrays)),
        scratch_shapes=[
            pltpu.SemaphoreType.DMA((len(arrays), n)),
            pltpu.SemaphoreType.DMA((len(arrays), n)),
            pltpu.SemaphoreType.DMA((len(arrays),)),
        ],
        compiler_params=pltpu.CompilerParams(collective_id=tag, has_side_effects=True),
        cost_estimate=pl.CostEstimate(flops=0, transcendentals=0, bytes_accessed=2 * moved),
    )(*arrays)


def per_device(
    tokens, value_weight, down_panels, up_panels, cotangent, block_adapter, adapter_slot
):
    n_owners = lax.axis_size("dp")
    myself = lax.axis_index("dp")
    n_split = lax.axis_size("mp")
    my_part = lax.axis_index("mp")
    rows, width_dev = tokens.shape
    own_rows, kv_full = cotangent.shape
    kv_part = kv_full // n_split
    stored = down_panels.shape[0]
    blocks = rows // BLOCK_ROWS
    hits = block_adapter[:, None] == jnp.arange(adapter_slot.shape[0], dtype=jnp.int32)[None, :]
    slots_all = jnp.sum(jnp.where(hits, adapter_slot[None, :], 0), axis=1)
    owner_all = (slots_all // stored).reshape(n_owners, blocks)
    local_all = (slots_all % stored).reshape(n_owners, blocks)
    mine = owner_all == myself
    wanted = jnp.sum(jnp.where(mine, local_all, 0), axis=1)
    served = jnp.any(mine, axis=1)
    pick_mask = (wanted[:, None] == jnp.arange(stored, dtype=jnp.int32)[None, :]) & served[:, None]
    my_owner = lax.dynamic_index_in_dim(owner_all, myself, 0, keepdims=False)
    select_mask = my_owner[:, None] == jnp.arange(n_owners, dtype=jnp.int32)[None, :]

    up_cols = lax.dynamic_slice_in_dim(up_panels, my_part * kv_part, kv_part, 2)
    both = jnp.concatenate([down_panels, up_cols], axis=1)
    got = lax.all_to_all(jnp.take(both, wanted, axis=0), "dp", split_axis=0, concat_axis=0, tiled=True)
    mine_got = jnp.take(got, my_owner, axis=0)
    panel_a = mine_got[:, :width_dev]
    panel_b_cols = mine_got[:, width_dev:]
    cot_all = lax.all_gather(cotangent, "mp", axis=0, tiled=True)

    token_blocks = tokens.reshape(blocks, BLOCK_ROWS, width_dev)
    partial_value = jnp.dot(tokens, value_weight, preferred_element_type=jnp.float32)
    base = lax.psum_scatter(partial_value, "mp", scatter_dimension=0, tiled=True)
    down_part = jnp.einsum(
        "bnd,bdk->bnk", token_blocks, panel_a, preferred_element_type=jnp.float32
    )
    part_block = (jnp.arange(n_split, dtype=jnp.int32) * own_rows) // BLOCK_ROWS
    to_parts = jnp.take(panel_b_cols, part_block, axis=0)
    down_parts, up_parts = mp_exchange(
        [down_part.reshape(n_split, own_rows, RANK), to_parts], [False, False], n_split, 0
    )
    my_down = jnp.sum(down_parts, axis=0).astype(jnp.bfloat16)
    my_up = up_parts.transpose(1, 0, 2).reshape(RANK, kv_full)
    my_back = jnp.einsum(
        "nc,kc->nk", cotangent, my_up, preferred_element_type=jnp.float32
    ).astype(jnp.bfloat16)
    down, back = mp_exchange([my_down[None], my_back[None]], [True, True], n_split, 1)
    down = down.reshape(rows, RANK).astype(jnp.bfloat16)
    back = back.reshape(blocks, BLOCK_ROWS, RANK)
    lifted = jnp.dot(my_down, my_up, preferred_element_type=jnp.float32)
    projected = (base + lifted).astype(jnp.bfloat16)

    cot_blocks = cot_all.reshape(blocks, BLOCK_ROWS, kv_full)
    block_grad_a = jnp.einsum(
        "bnd,bnk->bdk", token_blocks, back, preferred_element_type=jnp.float32
    ).astype(jnp.bfloat16)
    cot_share = lax.dynamic_slice_in_dim(cot_blocks, my_part * kv_part, kv_part, 2)
    block_grad_b = jnp.einsum(
        "bnk,bnc->bkc", down.reshape(blocks, BLOCK_ROWS, RANK), cot_share,
        preferred_element_type=jnp.float32,
    ).astype(jnp.bfloat16)
    grads = jnp.concatenate([block_grad_a, block_grad_b], axis=1)
    send_g = jnp.einsum(
        "bo,bdk->odk", select_mask.astype(jnp.bfloat16), grads, preferred_element_type=jnp.float32
    ).astype(jnp.bfloat16)
    recv_g = lax.all_to_all(send_g, "dp", split_axis=0, concat_axis=0, tiled=True)
    grad_both = jnp.einsum(
        "ra,rdk->adk", pick_mask.astype(jnp.bfloat16), recv_g, preferred_element_type=jnp.float32
    ).astype(jnp.bfloat16)
    grad_down = grad_both[:, :width_dev]
    grad_up = lax.all_gather(grad_both[:, width_dev:], "mp", axis=2, tiled=True)

    grad_base = jnp.einsum("nc,dc->nd", cot_all, value_weight, preferred_element_type=jnp.float32)
    through = jnp.einsum("bnk,bdk->bnd", back, panel_a, preferred_element_type=jnp.float32)
    grad_tokens = (grad_base + through.reshape(rows, width_dev)).astype(jnp.bfloat16)
    return (projected, grad_tokens, grad_down, grad_up)


def solution(mesh):
    placed = (
        P("dp", "mp"),
        P("mp", None),
        P("dp", "mp", None),
        P("dp", None, None),
        P(("dp", "mp"), None),
        P(),
        P(),
    )
    return jax.shard_map(
        per_device,
        mesh=mesh,
        in_specs=placed,
        out_specs=(P(("dp", "mp"), None), P("dp", "mp"), P("dp", "mp", None), P("dp", None, None)),
        check_vma=False,
    )
```

```python
import functools

import jax
import jax.numpy as jnp
from jax import lax
from jax.experimental import pallas as pl
from jax.experimental.pallas import tpu as pltpu
from jax.sharding import PartitionSpec as P

RANK = 64
BLOCK_ROWS = 128


def _exchange_kernel(n, spread, *refs):
    k = len(spread)
    ins, outs = refs[:k], refs[k:2 * k]
    send_sems, recv_sems, local_sem = refs[2 * k:]
    me = lax.axis_index("mp")
    row = lax.axis_index("dp")
    barrier = pltpu.get_barrier_semaphore()
    for d in range(1, n):
        pl.semaphore_signal(
            barrier, inc=1, device_id=(row, lax.rem(me + d, n)),
            device_id_type=pl.DeviceIdType.MESH,
        )
    pl.semaphore_wait(barrier, n - 1)
    copies = []
    for a in range(k):
        for d in range(1, n):
            tgt = lax.rem(me + d, n)
            src = ins[a].at[0] if spread[a] else ins[a].at[tgt]
            copy = pltpu.make_async_remote_copy(
                src_ref=src,
                dst_ref=outs[a].at[me],
                send_sem=send_sems.at[a, d],
                recv_sem=recv_sems.at[a, d],
                device_id=(row, tgt),
                device_id_type=pl.DeviceIdType.MESH,
            )
            copy.start()
            copies.append((a, d, copy))
    for a in range(k):
        src = ins[a].at[0] if spread[a] else ins[a].at[me]
        local = pltpu.make_async_copy(src, outs[a].at[me], local_sem.at[a])
        local.start()
        local.wait()
    for a, d, copy in copies:
        copy.wait_send()
        origin = lax.rem(me + n - d, n)
        pltpu.make_async_remote_copy(
            src_ref=outs[a].at[origin],
            dst_ref=outs[a].at[origin],
            send_sem=send_sems.at[a, d],
            recv_sem=recv_sems.at[a, d],
            device_id=(row, origin),
            device_id_type=pl.DeviceIdType.MESH,
        ).wait_recv()


def mp_exchange(arrays, spread, n, tag):
    outs = tuple(
        jax.ShapeDtypeStruct((n,) + x.shape[1:], x.dtype) for x in arrays
    )
    moved = sum(x.size * x.dtype.itemsize for x in outs)
    vmem = pl.BlockSpec(memory_space=pltpu.VMEM)
    return pl.pallas_call(
        functools.partial(_exchange_kernel, n, tuple(spread)),
        out_shape=outs,
        in_specs=[vmem] * len(arrays),
        out_specs=tuple([vmem] * len(arrays)),
        scratch_shapes=[
            pltpu.SemaphoreType.DMA((len(arrays), n)),
            pltpu.SemaphoreType.DMA((len(arrays), n)),
            pltpu.SemaphoreType.DMA((len(arrays),)),
        ],
        compiler_params=pltpu.CompilerParams(collective_id=tag, has_side_effects=True),
        cost_estimate=pl.CostEstimate(flops=0, transcendentals=0, bytes_accessed=2 * moved),
    )(*arrays)


def per_device(
    tokens, value_weight, down_panels, up_panels, cotangent, block_adapter, adapter_slot
):
    n_owners = lax.axis_size("dp")
    myself = lax.axis_index("dp")
    n_split = lax.axis_size("mp")
    my_part = lax.axis_index("mp")
    rows, width_dev = tokens.shape
    own_rows, kv_full = cotangent.shape
    kv_part = kv_full // n_split
    stored = down_panels.shape[0]
    blocks = rows // BLOCK_ROWS
    hits = block_adapter[:, None] == jnp.arange(adapter_slot.shape[0], dtype=jnp.int32)[None, :]
    slots_all = jnp.sum(jnp.where(hits, adapter_slot[None, :], 0), axis=1)
    owner_all = (slots_all // stored).reshape(n_owners, blocks)
    local_all = (slots_all % stored).reshape(n_owners, blocks)
    mine = owner_all == myself
    wanted = jnp.sum(jnp.where(mine, local_all, 0), axis=1)
    served = jnp.any(mine, axis=1)
    pick_mask = (wanted[:, None] == jnp.arange(stored, dtype=jnp.int32)[None, :]) & served[:, None]
    my_owner = lax.dynamic_index_in_dim(owner_all, myself, 0, keepdims=False)
    select_mask = my_owner[:, None] == jnp.arange(n_owners, dtype=jnp.int32)[None, :]

    up_cols = lax.dynamic_slice_in_dim(up_panels, my_part * kv_part, kv_part, 2)
    both = jnp.concatenate([down_panels, up_cols], axis=1)
    got = lax.all_to_all(jnp.take(both, wanted, axis=0), "dp", split_axis=0, concat_axis=0, tiled=True)
    mine_got = jnp.take(got, my_owner, axis=0)
    panel_a = mine_got[:, :width_dev]
    panel_b_cols = mine_got[:, width_dev:]
    ahead, behind = [cotangent], [cotangent]
    to_right = [(i, (i + 1) % n_split) for i in range(n_split)]
    to_left = [(i, (i - 1) % n_split) for i in range(n_split)]
    for step in range(n_split // 2):
        ahead.append(lax.ppermute(ahead[-1], "mp", to_right))
        if step < n_split // 2 - 1:
            behind.append(lax.ppermute(behind[-1], "mp", to_left))
    by_offset = [cotangent] + behind[1:] + ahead[:0:-1]
    stacked = jnp.concatenate(by_offset + by_offset, axis=0)
    cot_all = lax.dynamic_slice_in_dim(stacked, (n_split - my_part) * own_rows, rows, 0)

    token_blocks = tokens.reshape(blocks, BLOCK_ROWS, width_dev)
    partial_value = jnp.dot(tokens, value_weight, preferred_element_type=jnp.float32)
    base = lax.psum_scatter(partial_value, "mp", scatter_dimension=0, tiled=True)
    down_part = jnp.einsum(
        "bnd,bdk->bnk", token_blocks, panel_a, preferred_element_type=jnp.float32
    )
    part_block = (jnp.arange(n_split, dtype=jnp.int32) * own_rows) // BLOCK_ROWS
    to_parts = jnp.take(panel_b_cols, part_block, axis=0)
    down_parts, up_parts = mp_exchange(
        [down_part.reshape(n_split, own_rows, RANK), to_parts], [False, False], n_split, 0
    )
    my_down = jnp.sum(down_parts, axis=0).astype(jnp.bfloat16)
    my_up = up_parts.transpose(1, 0, 2).reshape(RANK, kv_full)
    my_back = jnp.einsum(
        "nc,kc->nk", cotangent, my_up, preferred_element_type=jnp.float32
    ).astype(jnp.bfloat16)
    base, my_down, my_back = lax.optimization_barrier((base, my_down, my_back))
    down, back = mp_exchange([my_down[None], my_back[None]], [True, True], n_split, 1)
    down = down.reshape(rows, RANK).astype(jnp.bfloat16)
    back = back.reshape(blocks, BLOCK_ROWS, RANK)
    lifted = jnp.dot(my_down, my_up, preferred_element_type=jnp.float32)
    projected = (base + lifted).astype(jnp.bfloat16)

    cot_blocks = cot_all.reshape(blocks, BLOCK_ROWS, kv_full)
    select_bf = select_mask.astype(jnp.bfloat16)
    pick_bf = pick_mask.astype(jnp.bfloat16)
    cot_share = lax.dynamic_slice_in_dim(cot_blocks, my_part * kv_part, kv_part, 2)
    block_grad_b = jnp.einsum(
        "bnk,bnc->bkc", down.reshape(blocks, BLOCK_ROWS, RANK), cot_share,
        preferred_element_type=jnp.float32,
    ).astype(jnp.bfloat16)
    send_gb = jnp.einsum(
        "bo,bkc->okc", select_bf, block_grad_b, preferred_element_type=jnp.float32
    ).astype(jnp.bfloat16)
    recv_gb = lax.all_to_all(send_gb, "dp", split_axis=0, concat_axis=0, tiled=True)
    grad_share = jnp.einsum(
        "ra,rkc->akc", pick_bf, recv_gb, preferred_element_type=jnp.float32
    ).astype(jnp.bfloat16)
    grad_up = lax.all_gather(grad_share, "mp", axis=2, tiled=True)

    block_grad_a = jnp.einsum(
        "bnd,bnk->bdk", token_blocks, back, preferred_element_type=jnp.float32
    ).astype(jnp.bfloat16)
    send_ga = jnp.einsum(
        "bo,bdk->odk", select_bf, block_grad_a, preferred_element_type=jnp.float32
    ).astype(jnp.bfloat16)
    recv_ga = lax.all_to_all(send_ga, "dp", split_axis=0, concat_axis=0, tiled=True)
    grad_down = jnp.einsum(
        "ra,rdk->adk", pick_bf, recv_ga, preferred_element_type=jnp.float32
    ).astype(jnp.bfloat16)

    grad_base = jnp.einsum("nc,dc->nd", cot_all, value_weight, preferred_element_type=jnp.float32)
    through = jnp.einsum("bnk,bdk->bnd", back, panel_a, preferred_element_type=jnp.float32)
    grad_tokens = (grad_base + through.reshape(rows, width_dev)).astype(jnp.bfloat16)
    return (projected, grad_tokens, grad_down, grad_up)


def solution(mesh):
    placed = (
        P("dp", "mp"),
        P("mp", None),
        P("dp", "mp", None),
        P("dp", None, None),
        P(("dp", "mp"), None),
        P(),
        P(),
    )
    return jax.shard_map(
        per_device,
        mesh=mesh,
        in_specs=placed,
        out_specs=(P(("dp", "mp"), None), P("dp", "mp"), P("dp", "mp", None), P("dp", None, None)),
        check_vma=False,
    )
```

```python
import functools

import jax
import jax.numpy as jnp
from jax import lax
from jax.experimental import pallas as pl
from jax.experimental.pallas import tpu as pltpu
from jax.sharding import PartitionSpec as P

RANK = 64
BLOCK_ROWS = 128


def _exchange_kernel(n, spread, *refs):
    k = len(spread)
    ins, outs = refs[:k], refs[k:2 * k]
    send_sems, recv_sems, local_sem = refs[2 * k:]
    me = lax.axis_index("mp")
    row = lax.axis_index("dp")
    barrier = pltpu.get_barrier_semaphore()
    for d in range(1, n):
        pl.semaphore_signal(
            barrier, inc=1, device_id=(row, lax.rem(me + d, n)),
            device_id_type=pl.DeviceIdType.MESH,
        )
    pl.semaphore_wait(barrier, n - 1)
    copies = []
    for a in range(k):
        for d in range(1, n):
            tgt = lax.rem(me + d, n)
            src = ins[a].at[0] if spread[a] else ins[a].at[tgt]
            copy = pltpu.make_async_remote_copy(
                src_ref=src,
                dst_ref=outs[a].at[me],
                send_sem=send_sems.at[a, d],
                recv_sem=recv_sems.at[a, d],
                device_id=(row, tgt),
                device_id_type=pl.DeviceIdType.MESH,
            )
            copy.start()
            copies.append((a, d, copy))
    for a in range(k):
        src = ins[a].at[0] if spread[a] else ins[a].at[me]
        local = pltpu.make_async_copy(src, outs[a].at[me], local_sem.at[a])
        local.start()
        local.wait()
    for a, d, copy in copies:
        copy.wait_send()
        origin = lax.rem(me + n - d, n)
        pltpu.make_async_remote_copy(
            src_ref=outs[a].at[origin],
            dst_ref=outs[a].at[origin],
            send_sem=send_sems.at[a, d],
            recv_sem=recv_sems.at[a, d],
            device_id=(row, origin),
            device_id_type=pl.DeviceIdType.MESH,
        ).wait_recv()


def mp_exchange(arrays, spread, n, tag):
    outs = tuple(
        jax.ShapeDtypeStruct((n,) + x.shape[1:], x.dtype) for x in arrays
    )
    moved = sum(x.size * x.dtype.itemsize for x in outs)
    vmem = pl.BlockSpec(memory_space=pltpu.VMEM)
    return pl.pallas_call(
        functools.partial(_exchange_kernel, n, tuple(spread)),
        out_shape=outs,
        in_specs=[vmem] * len(arrays),
        out_specs=tuple([vmem] * len(arrays)),
        scratch_shapes=[
            pltpu.SemaphoreType.DMA((len(arrays), n)),
            pltpu.SemaphoreType.DMA((len(arrays), n)),
            pltpu.SemaphoreType.DMA((len(arrays),)),
        ],
        compiler_params=pltpu.CompilerParams(collective_id=tag, has_side_effects=True),
        cost_estimate=pl.CostEstimate(flops=0, transcendentals=0, bytes_accessed=2 * moved),
    )(*arrays)


def per_device(
    tokens, value_weight, down_panels, up_panels, cotangent, block_adapter, adapter_slot
):
    n_owners = lax.axis_size("dp")
    myself = lax.axis_index("dp")
    n_split = lax.axis_size("mp")
    my_part = lax.axis_index("mp")
    rows, width_dev = tokens.shape
    own_rows, kv_full = cotangent.shape
    kv_part = kv_full // n_split
    stored = down_panels.shape[0]
    blocks = rows // BLOCK_ROWS
    hits = block_adapter[:, None] == jnp.arange(adapter_slot.shape[0], dtype=jnp.int32)[None, :]
    slots_all = jnp.sum(jnp.where(hits, adapter_slot[None, :], 0), axis=1)
    owner_all = (slots_all // stored).reshape(n_owners, blocks)
    local_all = (slots_all % stored).reshape(n_owners, blocks)
    mine = owner_all == myself
    wanted = jnp.sum(jnp.where(mine, local_all, 0), axis=1)
    served = jnp.any(mine, axis=1)
    pick_mask = (wanted[:, None] == jnp.arange(stored, dtype=jnp.int32)[None, :]) & served[:, None]
    my_owner = lax.dynamic_index_in_dim(owner_all, myself, 0, keepdims=False)
    select_mask = my_owner[:, None] == jnp.arange(n_owners, dtype=jnp.int32)[None, :]

    up_cols = lax.dynamic_slice_in_dim(up_panels, my_part * kv_part, kv_part, 2)
    both = jnp.concatenate([down_panels, up_cols], axis=1)
    got = lax.all_to_all(jnp.take(both, wanted, axis=0), "dp", split_axis=0, concat_axis=0, tiled=True)
    mine_got = jnp.take(got, my_owner, axis=0)
    panel_a = mine_got[:, :width_dev]
    panel_b_cols = mine_got[:, width_dev:]
    (cot_all,) = mp_exchange([cotangent[None]], [True], n_split, 2)
    cot_all = cot_all.reshape(rows, kv_full)

    token_blocks = tokens.reshape(blocks, BLOCK_ROWS, width_dev)
    partial_value = jnp.dot(tokens, value_weight, preferred_element_type=jnp.float32)
    base = lax.psum_scatter(partial_value, "mp", scatter_dimension=0, tiled=True)
    down_part = jnp.einsum(
        "bnd,bdk->bnk", token_blocks, panel_a, preferred_element_type=jnp.float32
    )
    part_block = (jnp.arange(n_split, dtype=jnp.int32) * own_rows) // BLOCK_ROWS
    to_parts = jnp.take(panel_b_cols, part_block, axis=0)
    down_parts, up_parts = mp_exchange(
        [down_part.reshape(n_split, own_rows, RANK), to_parts], [False, False], n_split, 0
    )
    my_down = jnp.sum(down_parts, axis=0).astype(jnp.bfloat16)
    my_up = up_parts.transpose(1, 0, 2).reshape(RANK, kv_full)
    my_back = jnp.einsum(
        "nc,kc->nk", cotangent, my_up, preferred_element_type=jnp.float32
    ).astype(jnp.bfloat16)
    base, my_down, my_back = lax.optimization_barrier((base, my_down, my_back))
    down, back = mp_exchange([my_down[None], my_back[None]], [True, True], n_split, 1)
    down = down.reshape(rows, RANK).astype(jnp.bfloat16)
    back = back.reshape(blocks, BLOCK_ROWS, RANK)
    lifted = jnp.dot(my_down, my_up, preferred_element_type=jnp.float32)
    projected = (base + lifted).astype(jnp.bfloat16)

    cot_blocks = cot_all.reshape(blocks, BLOCK_ROWS, kv_full)
    select_bf = select_mask.astype(jnp.bfloat16)
    pick_bf = pick_mask.astype(jnp.bfloat16)
    cot_share = lax.dynamic_slice_in_dim(cot_blocks, my_part * kv_part, kv_part, 2)
    block_grad_b = jnp.einsum(
        "bnk,bnc->bkc", down.reshape(blocks, BLOCK_ROWS, RANK), cot_share,
        preferred_element_type=jnp.float32,
    ).astype(jnp.bfloat16)
    send_gb = jnp.einsum(
        "bo,bkc->okc", select_bf, block_grad_b, preferred_element_type=jnp.float32
    ).astype(jnp.bfloat16)
    recv_gb = lax.all_to_all(send_gb, "dp", split_axis=0, concat_axis=0, tiled=True)
    grad_share = jnp.einsum(
        "ra,rkc->akc", pick_bf, recv_gb, preferred_element_type=jnp.float32
    ).astype(jnp.bfloat16)
    grad_up = lax.all_gather(grad_share, "mp", axis=2, tiled=True)

    block_grad_a = jnp.einsum(
        "bnd,bnk->bdk", token_blocks, back, preferred_element_type=jnp.float32
    ).astype(jnp.bfloat16)
    send_ga = jnp.einsum(
        "bo,bdk->odk", select_bf, block_grad_a, preferred_element_type=jnp.float32
    ).astype(jnp.bfloat16)
    recv_ga = lax.all_to_all(send_ga, "dp", split_axis=0, concat_axis=0, tiled=True)
    grad_down = jnp.einsum(
        "ra,rdk->adk", pick_bf, recv_ga, preferred_element_type=jnp.float32
    ).astype(jnp.bfloat16)

    grad_base = jnp.einsum("nc,dc->nd", cot_all, value_weight, preferred_element_type=jnp.float32)
    through = jnp.einsum("bnk,bdk->bnd", back, panel_a, preferred_element_type=jnp.float32)
    grad_tokens = (grad_base + through.reshape(rows, width_dev)).astype(jnp.bfloat16)
    return (projected, grad_tokens, grad_down, grad_up)


def solution(mesh):
    placed = (
        P("dp", "mp"),
        P("mp", None),
        P("dp", "mp", None),
        P("dp", None, None),
        P(("dp", "mp"), None),
        P(),
        P(),
    )
    return jax.shard_map(
        per_device,
        mesh=mesh,
        in_specs=placed,
        out_specs=(P(("dp", "mp"), None), P("dp", "mp"), P("dp", "mp", None), P("dp", None, None)),
        check_vma=False,
    )
```

```python
import functools

import jax
import jax.numpy as jnp
from jax import lax
from jax.experimental import pallas as pl
from jax.experimental.pallas import tpu as pltpu
from jax.sharding import PartitionSpec as P

RANK = 64
BLOCK_ROWS = 128


def _ring_kernel(n, k, *refs):
    ins, outs = refs[:k], refs[k:2 * k]
    send_sems, recv_sems, local_sem = refs[2 * k:]
    me = lax.axis_index("mp")
    row = lax.axis_index("dp")
    right = lax.rem(me + 1, n)
    left = lax.rem(me + n - 1, n)
    barrier = pltpu.get_barrier_semaphore()
    for peer in (left, right):
        pl.semaphore_signal(
            barrier, inc=1, device_id=(row, peer), device_id_type=pl.DeviceIdType.MESH
        )
    pl.semaphore_wait(barrier, 2)
    for a in range(k):
        local = pltpu.make_async_copy(ins[a].at[0], outs[a].at[me], local_sem.at[a])
        local.start()
        local.wait()
    reach = (n // 2, n - 1 - n // 2)
    streams = ((0, right, -1), (1, left, 1))

    def link(a, way, step, slot, peer):
        return pltpu.make_async_remote_copy(
            src_ref=outs[a].at[slot],
            dst_ref=outs[a].at[slot],
            send_sem=send_sems.at[a, way, step],
            recv_sem=recv_sems.at[a, way, step],
            device_id=(row, peer),
            device_id_type=pl.DeviceIdType.MESH,
        )

    started = []
    for step in range(1, reach[0] + 1):
        for way, peer, sign in streams:
            if step > reach[way]:
                continue
            slot = lax.rem(me + n + sign * (step - 1), n)
            for a in range(k):
                if step > 1:
                    link(a, way, step - 1, slot, peer).wait_recv()
                copy = link(a, way, step, slot, peer)
                copy.start()
                started.append(copy)
    for way, peer, sign in streams:
        last = reach[way]
        slot = lax.rem(me + n + sign * last, n)
        for a in range(k):
            link(a, way, last, slot, peer).wait_recv()
    for copy in started:
        copy.wait_send()


def ring_gather(arrays, n, tag):
    outs = tuple(jax.ShapeDtypeStruct((n,) + x.shape[1:], x.dtype) for x in arrays)
    moved = sum(x.size * x.dtype.itemsize for x in outs)
    vmem = pl.BlockSpec(memory_space=pltpu.VMEM)
    k = len(arrays)
    return pl.pallas_call(
        functools.partial(_ring_kernel, n, k),
        out_shape=outs,
        in_specs=[vmem] * k,
        out_specs=tuple([vmem] * k),
        scratch_shapes=[
            pltpu.SemaphoreType.DMA((k, 2, n // 2 + 1)),
            pltpu.SemaphoreType.DMA((k, 2, n // 2 + 1)),
            pltpu.SemaphoreType.DMA((k,)),
        ],
        compiler_params=pltpu.CompilerParams(collective_id=tag, has_side_effects=True),
        cost_estimate=pl.CostEstimate(flops=0, transcendentals=0, bytes_accessed=2 * moved),
    )(*arrays)


def per_device(
    tokens, value_weight, down_panels, up_panels, cotangent, block_adapter, adapter_slot
):
    n_owners = lax.axis_size("dp")
    myself = lax.axis_index("dp")
    n_split = lax.axis_size("mp")
    my_part = lax.axis_index("mp")
    rows, width_dev = tokens.shape
    own_rows, kv_full = cotangent.shape
    kv_part = kv_full // n_split
    stored = down_panels.shape[0]
    blocks = rows // BLOCK_ROWS
    hits = block_adapter[:, None] == jnp.arange(adapter_slot.shape[0], dtype=jnp.int32)[None, :]
    slots_all = jnp.sum(jnp.where(hits, adapter_slot[None, :], 0), axis=1)
    owner_all = (slots_all // stored).reshape(n_owners, blocks)
    local_all = (slots_all % stored).reshape(n_owners, blocks)
    mine = owner_all == myself
    wanted = jnp.sum(jnp.where(mine, local_all, 0), axis=1)
    served = jnp.any(mine, axis=1)
    pick_mask = (wanted[:, None] == jnp.arange(stored, dtype=jnp.int32)[None, :]) & served[:, None]
    my_owner = lax.dynamic_index_in_dim(owner_all, myself, 0, keepdims=False)
    select_mask = my_owner[:, None] == jnp.arange(n_owners, dtype=jnp.int32)[None, :]

    up_cols = lax.dynamic_slice_in_dim(up_panels, my_part * kv_part, kv_part, 2)
    both = jnp.concatenate([down_panels, up_cols], axis=1)
    got = lax.all_to_all(jnp.take(both, wanted, axis=0), "dp", split_axis=0, concat_axis=0, tiled=True)
    mine_got = jnp.take(got, my_owner, axis=0)
    panel_a = mine_got[:, :width_dev]
    panel_b_cols = mine_got[:, width_dev:]
    (cot_all,) = ring_gather([cotangent[None]], n_split, 0)
    cot_all = cot_all.reshape(rows, kv_full)
    cot_blocks = cot_all.reshape(blocks, BLOCK_ROWS, kv_full)

    token_blocks = tokens.reshape(blocks, BLOCK_ROWS, width_dev)
    partial_value = jnp.dot(tokens, value_weight, preferred_element_type=jnp.float32)
    base = lax.psum_scatter(partial_value, "mp", scatter_dimension=0, tiled=True)
    down_part = jnp.einsum(
        "bnd,bdk->bnk", token_blocks, panel_a, preferred_element_type=jnp.float32
    ).astype(jnp.bfloat16)
    parts_down, parts_up = ring_gather([down_part[None], panel_b_cols[None]], n_split, 1)
    down = jnp.sum(parts_down.astype(jnp.float32), axis=0).astype(jnp.bfloat16)
    panel_b = parts_up.transpose(1, 2, 0, 3).reshape(blocks, RANK, kv_full)
    back = jnp.einsum(
        "bnc,bkc->bnk", cot_blocks, panel_b, preferred_element_type=jnp.float32
    ).astype(jnp.bfloat16)

    first_row = my_part * own_rows
    my_down = lax.dynamic_slice_in_dim(down.reshape(rows, RANK), first_row, own_rows, 0)
    my_up = lax.dynamic_index_in_dim(panel_b, first_row // BLOCK_ROWS, 0, keepdims=False)
    lifted = jnp.dot(my_down, my_up, preferred_element_type=jnp.float32)
    projected = (base + lifted).astype(jnp.bfloat16)

    select_bf = select_mask.astype(jnp.bfloat16)
    pick_bf = pick_mask.astype(jnp.bfloat16)
    cot_share = lax.dynamic_slice_in_dim(cot_blocks, my_part * kv_part, kv_part, 2)
    block_grad_b = jnp.einsum(
        "bnk,bnc->bkc", down, cot_share, preferred_element_type=jnp.float32
    ).astype(jnp.bfloat16)
    send_gb = jnp.einsum(
        "bo,bkc->okc", select_bf, block_grad_b, preferred_element_type=jnp.float32
    ).astype(jnp.bfloat16)
    recv_gb = lax.all_to_all(send_gb, "dp", split_axis=0, concat_axis=0, tiled=True)
    grad_share = jnp.einsum(
        "ra,rkc->akc", pick_bf, recv_gb, preferred_element_type=jnp.float32
    ).astype(jnp.bfloat16)

    block_grad_a = jnp.einsum(
        "bnd,bnk->bdk", token_blocks, back, preferred_element_type=jnp.float32
    ).astype(jnp.bfloat16)
    send_ga = jnp.einsum(
        "bo,bdk->odk", select_bf, block_grad_a, preferred_element_type=jnp.float32
    ).astype(jnp.bfloat16)
    recv_ga = lax.all_to_all(send_ga, "dp", split_axis=0, concat_axis=0, tiled=True)
    grad_down = jnp.einsum(
        "ra,rdk->adk", pick_bf, recv_ga, preferred_element_type=jnp.float32
    ).astype(jnp.bfloat16)
    (shares,) = ring_gather([grad_share[None]], n_split, 2)
    grad_up = shares.transpose(1, 2, 0, 3).reshape(stored, RANK, kv_full)

    grad_base = jnp.einsum("nc,dc->nd", cot_all, value_weight, preferred_element_type=jnp.float32)
    through = jnp.einsum("bnk,bdk->bnd", back, panel_a, preferred_element_type=jnp.float32)
    grad_tokens = (grad_base + through.reshape(rows, width_dev)).astype(jnp.bfloat16)
    return (projected, grad_tokens, grad_down, grad_up)


def solution(mesh):
    placed = (
        P("dp", "mp"),
        P("mp", None),
        P("dp", "mp", None),
        P("dp", None, None),
        P(("dp", "mp"), None),
        P(),
        P(),
    )
    return jax.shard_map(
        per_device,
        mesh=mesh,
        in_specs=placed,
        out_specs=(P(("dp", "mp"), None), P("dp", "mp"), P("dp", "mp", None), P("dp", None, None)),
        check_vma=False,
    )
```

```python
import functools

import jax
import jax.numpy as jnp
from jax import lax
from jax.experimental import pallas as pl
from jax.experimental.pallas import tpu as pltpu
from jax.sharding import PartitionSpec as P

RANK = 64
BLOCK_ROWS = 128


def _ring_kernel(n, k, pieces, *refs):
    ins, outs = refs[:k], refs[k:2 * k]
    send_sems, recv_sems, local_sem = refs[2 * k:]
    me = lax.axis_index("mp")
    row = lax.axis_index("dp")
    right = lax.rem(me + 1, n)
    left = lax.rem(me + n - 1, n)
    barrier = pltpu.get_barrier_semaphore()
    for peer in (left, right):
        pl.semaphore_signal(
            barrier, inc=1, device_id=(row, peer), device_id_type=pl.DeviceIdType.MESH
        )
    pl.semaphore_wait(barrier, 2)
    for a in range(k):
        local = pltpu.make_async_copy(ins[a].at[0], outs[a].at[me], local_sem.at[a])
        local.start()
        local.wait()
    reach = (n // 2, n - 1 - n // 2)
    streams = ((0, right, -1), (1, left, 1))

    def link(a, way, step, slot, peer, i):
        size = outs[a].shape[1] // pieces
        part = outs[a].at[slot, pl.ds(i * size, size)]
        return pltpu.make_async_remote_copy(
            src_ref=part,
            dst_ref=part,
            send_sem=send_sems.at[a, way, step, i],
            recv_sem=recv_sems.at[a, way, step, i],
            device_id=(row, peer),
            device_id_type=pl.DeviceIdType.MESH,
        )

    started = []
    for step in range(1, reach[0] + 1):
        for way, peer, sign in streams:
            if step > reach[way]:
                continue
            slot = lax.rem(me + n + sign * (step - 1), n)
            for a in range(k):
                for i in range(pieces):
                    if step > 1:
                        link(a, way, step - 1, slot, peer, i).wait_recv()
                    copy = link(a, way, step, slot, peer, i)
                    copy.start()
                    started.append(copy)
    for way, peer, sign in streams:
        last = reach[way]
        slot = lax.rem(me + n + sign * last, n)
        for a in range(k):
            for i in range(pieces):
                link(a, way, last, slot, peer, i).wait_recv()
    for copy in started:
        copy.wait_send()


def ring_gather(arrays, n, tag, pieces=4):
    outs = tuple(jax.ShapeDtypeStruct((n,) + x.shape[1:], x.dtype) for x in arrays)
    moved = sum(x.size * x.dtype.itemsize for x in outs)
    vmem = pl.BlockSpec(memory_space=pltpu.VMEM)
    k = len(arrays)
    return pl.pallas_call(
        functools.partial(_ring_kernel, n, k, pieces),
        out_shape=outs,
        in_specs=[vmem] * k,
        out_specs=tuple([vmem] * k),
        scratch_shapes=[
            pltpu.SemaphoreType.DMA((k, 2, n // 2 + 1, pieces)),
            pltpu.SemaphoreType.DMA((k, 2, n // 2 + 1, pieces)),
            pltpu.SemaphoreType.DMA((k,)),
        ],
        compiler_params=pltpu.CompilerParams(collective_id=tag, has_side_effects=True),
        cost_estimate=pl.CostEstimate(flops=0, transcendentals=0, bytes_accessed=2 * moved),
    )(*arrays)


def per_device(
    tokens, value_weight, down_panels, up_panels, cotangent, block_adapter, adapter_slot
):
    n_owners = lax.axis_size("dp")
    myself = lax.axis_index("dp")
    n_split = lax.axis_size("mp")
    my_part = lax.axis_index("mp")
    rows, width_dev = tokens.shape
    own_rows, kv_full = cotangent.shape
    kv_part = kv_full // n_split
    stored = down_panels.shape[0]
    blocks = rows // BLOCK_ROWS
    hits = block_adapter[:, None] == jnp.arange(adapter_slot.shape[0], dtype=jnp.int32)[None, :]
    slots_all = jnp.sum(jnp.where(hits, adapter_slot[None, :], 0), axis=1)
    owner_all = (slots_all // stored).reshape(n_owners, blocks)
    local_all = (slots_all % stored).reshape(n_owners, blocks)
    mine = owner_all == myself
    wanted = jnp.sum(jnp.where(mine, local_all, 0), axis=1)
    served = jnp.any(mine, axis=1)
    pick_mask = (wanted[:, None] == jnp.arange(stored, dtype=jnp.int32)[None, :]) & served[:, None]
    my_owner = lax.dynamic_index_in_dim(owner_all, myself, 0, keepdims=False)
    select_mask = my_owner[:, None] == jnp.arange(n_owners, dtype=jnp.int32)[None, :]

    up_cols = lax.dynamic_slice_in_dim(up_panels, my_part * kv_part, kv_part, 2)
    both = jnp.concatenate([down_panels, up_cols], axis=1)
    got = lax.all_to_all(jnp.take(both, wanted, axis=0), "dp", split_axis=0, concat_axis=0, tiled=True)
    mine_got = jnp.take(got, my_owner, axis=0)
    panel_a = mine_got[:, :width_dev]
    panel_b_cols = mine_got[:, width_dev:]
    (cot_all,) = ring_gather([cotangent[None]], n_split, 0)
    cot_all = cot_all.reshape(rows, kv_full)
    cot_blocks = cot_all.reshape(blocks, BLOCK_ROWS, kv_full)

    token_blocks = tokens.reshape(blocks, BLOCK_ROWS, width_dev)
    partial_value = jnp.dot(tokens, value_weight, preferred_element_type=jnp.float32)
    base = lax.psum_scatter(partial_value, "mp", scatter_dimension=0, tiled=True)
    down_part = jnp.einsum(
        "bnd,bdk->bnk", token_blocks, panel_a, preferred_element_type=jnp.float32
    ).astype(jnp.bfloat16)
    parts_down, parts_up = ring_gather([down_part[None], panel_b_cols[None]], n_split, 1)
    down = jnp.sum(parts_down.astype(jnp.float32), axis=0).astype(jnp.bfloat16)
    panel_b = parts_up.transpose(1, 2, 0, 3).reshape(blocks, RANK, kv_full)
    back = jnp.einsum(
        "bnc,bkc->bnk", cot_blocks, panel_b, preferred_element_type=jnp.float32
    ).astype(jnp.bfloat16)

    first_row = my_part * own_rows
    my_down = lax.dynamic_slice_in_dim(down.reshape(rows, RANK), first_row, own_rows, 0)
    my_up = lax.dynamic_index_in_dim(panel_b, first_row // BLOCK_ROWS, 0, keepdims=False)
    lifted = jnp.dot(my_down, my_up, preferred_element_type=jnp.float32)
    projected = (base + lifted).astype(jnp.bfloat16)

    select_bf = select_mask.astype(jnp.bfloat16)
    pick_bf = pick_mask.astype(jnp.bfloat16)
    cot_share = lax.dynamic_slice_in_dim(cot_blocks, my_part * kv_part, kv_part, 2)
    block_grad_b = jnp.einsum(
        "bnk,bnc->bkc", down, cot_share, preferred_element_type=jnp.float32
    )
    send_gb = jnp.einsum(
        "bo,bkc->okc", select_mask.astype(jnp.float32), block_grad_b,
        precision=lax.Precision.HIGHEST,
    )
    recv_gb = lax.all_to_all(send_gb, "dp", split_axis=0, concat_axis=0, tiled=True)
    grad_share = jnp.einsum(
        "ra,rkc->akc", pick_mask.astype(jnp.float32), recv_gb, precision=lax.Precision.HIGHEST
    ).astype(jnp.bfloat16)

    block_grad_a = jnp.einsum(
        "bnd,bnk->bdk", token_blocks, back, preferred_element_type=jnp.float32
    ).astype(jnp.bfloat16)
    send_ga = jnp.einsum(
        "bo,bdk->odk", select_bf, block_grad_a, preferred_element_type=jnp.float32
    ).astype(jnp.bfloat16)
    recv_ga = lax.all_to_all(send_ga, "dp", split_axis=0, concat_axis=0, tiled=True)
    grad_down = jnp.einsum(
        "ra,rdk->adk", pick_bf, recv_ga, preferred_element_type=jnp.float32
    ).astype(jnp.bfloat16)
    (shares,) = ring_gather([grad_share[None]], n_split, 2)
    grad_up = shares.transpose(1, 2, 0, 3).reshape(stored, RANK, kv_full)

    grad_base = jnp.einsum("nc,dc->nd", cot_all, value_weight, preferred_element_type=jnp.float32)
    through = jnp.einsum("bnk,bdk->bnd", back, panel_a, preferred_element_type=jnp.float32)
    grad_tokens = (grad_base + through.reshape(rows, width_dev)).astype(jnp.bfloat16)
    return (projected, grad_tokens, grad_down, grad_up)


def solution(mesh):
    placed = (
        P("dp", "mp"),
        P("mp", None),
        P("dp", "mp", None),
        P("dp", None, None),
        P(("dp", "mp"), None),
        P(),
        P(),
    )
    return jax.shard_map(
        per_device,
        mesh=mesh,
        in_specs=placed,
        out_specs=(P(("dp", "mp"), None), P("dp", "mp"), P("dp", "mp", None), P("dp", None, None)),
        check_vma=False,
    )
```

```python
import functools

import jax
import jax.numpy as jnp
from jax import lax
from jax.experimental import pallas as pl
from jax.experimental.pallas import tpu as pltpu
from jax.sharding import PartitionSpec as P

RANK = 64
BLOCK_ROWS = 128


def _ring_kernel(n, k, pieces, *refs):
    ins, outs = refs[:k], refs[k:2 * k]
    send_sems, recv_sems, local_sem = refs[2 * k:]
    me = lax.axis_index("mp")
    row = lax.axis_index("dp")
    right = lax.rem(me + 1, n)
    left = lax.rem(me + n - 1, n)
    barrier = pltpu.get_barrier_semaphore()
    for peer in (left, right):
        pl.semaphore_signal(
            barrier, inc=1, device_id=(row, peer), device_id_type=pl.DeviceIdType.MESH
        )
    pl.semaphore_wait(barrier, 2)
    for a in range(k):
        local = pltpu.make_async_copy(ins[a].at[0], outs[a].at[me], local_sem.at[a])
        local.start()
        local.wait()
    reach = (n // 2, n - 1 - n // 2)
    streams = ((0, right, -1), (1, left, 1))

    def link(a, way, step, slot, peer, i):
        size = outs[a].shape[1] // pieces
        part = outs[a].at[slot, pl.ds(i * size, size)]
        return pltpu.make_async_remote_copy(
            src_ref=part,
            dst_ref=part,
            send_sem=send_sems.at[a, way, step, i],
            recv_sem=recv_sems.at[a, way, step, i],
            device_id=(row, peer),
            device_id_type=pl.DeviceIdType.MESH,
        )

    started = []
    for step in range(1, reach[0] + 1):
        for way, peer, sign in streams:
            if step > reach[way]:
                continue
            slot = lax.rem(me + n + sign * (step - 1), n)
            for a in range(k):
                for i in range(pieces):
                    if step > 1:
                        link(a, way, step - 1, slot, peer, i).wait_recv()
                    copy = link(a, way, step, slot, peer, i)
                    copy.start()
                    started.append(copy)
    for way, peer, sign in streams:
        last = reach[way]
        slot = lax.rem(me + n + sign * last, n)
        for a in range(k):
            for i in range(pieces):
                link(a, way, last, slot, peer, i).wait_recv()
    for copy in started:
        copy.wait_send()


def ring_gather(arrays, n, tag, pieces=4):
    outs = tuple(jax.ShapeDtypeStruct((n,) + x.shape[1:], x.dtype) for x in arrays)
    moved = sum(x.size * x.dtype.itemsize for x in outs)
    vmem = pl.BlockSpec(memory_space=pltpu.VMEM)
    k = len(arrays)
    return pl.pallas_call(
        functools.partial(_ring_kernel, n, k, pieces),
        out_shape=outs,
        in_specs=[vmem] * k,
        out_specs=tuple([vmem] * k),
        scratch_shapes=[
            pltpu.SemaphoreType.DMA((k, 2, n // 2 + 1, pieces)),
            pltpu.SemaphoreType.DMA((k, 2, n // 2 + 1, pieces)),
            pltpu.SemaphoreType.DMA((k,)),
        ],
        compiler_params=pltpu.CompilerParams(collective_id=tag, has_side_effects=True),
        cost_estimate=pl.CostEstimate(flops=0, transcendentals=0, bytes_accessed=2 * moved),
    )(*arrays)


def per_device(
    tokens, value_weight, down_panels, up_panels, cotangent, block_adapter, adapter_slot
):
    n_owners = lax.axis_size("dp")
    myself = lax.axis_index("dp")
    n_split = lax.axis_size("mp")
    my_part = lax.axis_index("mp")
    rows, width_dev = tokens.shape
    own_rows, kv_full = cotangent.shape
    kv_part = kv_full // n_split
    stored = down_panels.shape[0]
    blocks = rows // BLOCK_ROWS
    hits = block_adapter[:, None] == jnp.arange(adapter_slot.shape[0], dtype=jnp.int32)[None, :]
    slots_all = jnp.sum(jnp.where(hits, adapter_slot[None, :], 0), axis=1)
    owner_all = (slots_all // stored).reshape(n_owners, blocks)
    local_all = (slots_all % stored).reshape(n_owners, blocks)
    mine = owner_all == myself
    wanted = jnp.sum(jnp.where(mine, local_all, 0), axis=1)
    served = jnp.any(mine, axis=1)
    pick_mask = (wanted[:, None] == jnp.arange(stored, dtype=jnp.int32)[None, :]) & served[:, None]
    my_owner = lax.dynamic_index_in_dim(owner_all, myself, 0, keepdims=False)
    select_mask = my_owner[:, None] == jnp.arange(n_owners, dtype=jnp.int32)[None, :]

    up_cols = lax.dynamic_slice_in_dim(up_panels, my_part * kv_part, kv_part, 2)
    both = jnp.concatenate([down_panels, up_cols], axis=1)
    got = lax.all_to_all(jnp.take(both, wanted, axis=0), "dp", split_axis=0, concat_axis=0, tiled=True)
    mine_got = jnp.take(got, my_owner, axis=0)
    panel_a = mine_got[:, :width_dev]
    panel_b_cols = mine_got[:, width_dev:]
    (cot_all,) = ring_gather([cotangent[None]], n_split, 0)
    cot_all = cot_all.reshape(rows, kv_full)
    cot_blocks = cot_all.reshape(blocks, BLOCK_ROWS, kv_full)

    token_blocks = tokens.reshape(blocks, BLOCK_ROWS, width_dev)
    partial_value = jnp.dot(tokens, value_weight, preferred_element_type=jnp.float32)
    base = lax.psum_scatter(partial_value, "mp", scatter_dimension=0, tiled=True)
    down_part = jnp.einsum(
        "bnd,bdk->bnk", token_blocks, panel_a, preferred_element_type=jnp.float32
    ).astype(jnp.bfloat16)
    down_rows = down_part.size // kv_full
    packed = jnp.concatenate(
        [down_part.reshape(down_rows, kv_full), panel_b_cols.reshape(-1, kv_full)], axis=0
    )
    (parts,) = ring_gather([packed[None]], n_split, 1, pieces=3)
    down = jnp.sum(parts[:, :down_rows].astype(jnp.float32), axis=0)
    down = down.astype(jnp.bfloat16).reshape(blocks, BLOCK_ROWS, RANK)
    parts_up = parts[:, down_rows:].reshape(n_split, blocks, RANK, kv_part)
    panel_b = parts_up.transpose(1, 2, 0, 3).reshape(blocks, RANK, kv_full)
    back = jnp.einsum(
        "bnc,bkc->bnk", cot_blocks, panel_b, preferred_element_type=jnp.float32
    ).astype(jnp.bfloat16)

    first_row = my_part * own_rows
    my_down = lax.dynamic_slice_in_dim(down.reshape(rows, RANK), first_row, own_rows, 0)
    my_up = lax.dynamic_index_in_dim(panel_b, first_row // BLOCK_ROWS, 0, keepdims=False)
    lifted = jnp.dot(my_down, my_up, preferred_element_type=jnp.float32)
    projected = (base + lifted).astype(jnp.bfloat16)

    select_bf = select_mask.astype(jnp.bfloat16)
    pick_bf = pick_mask.astype(jnp.bfloat16)
    cot_share = lax.dynamic_slice_in_dim(cot_blocks, my_part * kv_part, kv_part, 2)
    block_grad_b = jnp.einsum(
        "bnk,bnc->bkc", down, cot_share, preferred_element_type=jnp.float32
    )
    send_gb = jnp.einsum(
        "bo,bkc->okc", select_mask.astype(jnp.float32), block_grad_b,
        precision=lax.Precision.HIGHEST,
    )
    recv_gb = lax.all_to_all(send_gb, "dp", split_axis=0, concat_axis=0, tiled=True)
    grad_share = jnp.einsum(
        "ra,rkc->akc", pick_mask.astype(jnp.float32), recv_gb, precision=lax.Precision.HIGHEST
    ).astype(jnp.bfloat16)

    block_grad_a = jnp.einsum(
        "bnd,bnk->bdk", token_blocks, back, preferred_element_type=jnp.float32
    ).astype(jnp.bfloat16)
    send_ga = jnp.einsum(
        "bo,bdk->odk", select_bf, block_grad_a, preferred_element_type=jnp.float32
    ).astype(jnp.bfloat16)
    recv_ga = lax.all_to_all(send_ga, "dp", split_axis=0, concat_axis=0, tiled=True)
    grad_down = jnp.einsum(
        "ra,rdk->adk", pick_bf, recv_ga, preferred_element_type=jnp.float32
    ).astype(jnp.bfloat16)
    (shares,) = ring_gather([grad_share.reshape(1, -1, kv_full)], n_split, 2, pieces=2)
    shares = shares.reshape(n_split, stored, RANK, kv_part)
    grad_up = shares.transpose(1, 2, 0, 3).reshape(stored, RANK, kv_full)

    grad_base = jnp.einsum("nc,dc->nd", cot_all, value_weight, preferred_element_type=jnp.float32)
    through = jnp.einsum("bnk,bdk->bnd", back, panel_a, preferred_element_type=jnp.float32)
    grad_tokens = (grad_base + through.reshape(rows, width_dev)).astype(jnp.bfloat16)
    return (projected, grad_tokens, grad_down, grad_up)


def solution(mesh):
    placed = (
        P("dp", "mp"),
        P("mp", None),
        P("dp", "mp", None),
        P("dp", None, None),
        P(("dp", "mp"), None),
        P(),
        P(),
    )
    return jax.shard_map(
        per_device,
        mesh=mesh,
        in_specs=placed,
        out_specs=(P(("dp", "mp"), None), P("dp", "mp"), P("dp", "mp", None), P("dp", None, None)),
        check_vma=False,
    )
```

```python
import functools

import jax
import jax.numpy as jnp
from jax import lax
from jax.experimental import pallas as pl
from jax.experimental.pallas import tpu as pltpu
from jax.sharding import PartitionSpec as P

RANK = 64
BLOCK_ROWS = 128


def _ring_kernel(n, k, pieces, *refs):
    ins, outs = refs[:k], refs[k:2 * k]
    send_sems, recv_sems, local_sem = refs[2 * k:]
    me = lax.axis_index("mp")
    row = lax.axis_index("dp")
    right = lax.rem(me + 1, n)
    left = lax.rem(me + n - 1, n)
    barrier = pltpu.get_barrier_semaphore()
    for peer in (left, right):
        pl.semaphore_signal(
            barrier, inc=1, device_id=(row, peer), device_id_type=pl.DeviceIdType.MESH
        )
    pl.semaphore_wait(barrier, 2)
    for a in range(k):
        local = pltpu.make_async_copy(ins[a].at[0], outs[a].at[me], local_sem.at[a])
        local.start()
        local.wait()
    reach = (n // 2, n - 1 - n // 2)
    streams = ((0, right, -1), (1, left, 1))

    def link(a, way, step, slot, peer, i):
        size = outs[a].shape[1] // pieces
        part = outs[a].at[slot, pl.ds(i * size, size)]
        return pltpu.make_async_remote_copy(
            src_ref=part,
            dst_ref=part,
            send_sem=send_sems.at[a, way, step, i],
            recv_sem=recv_sems.at[a, way, step, i],
            device_id=(row, peer),
            device_id_type=pl.DeviceIdType.MESH,
        )

    started = []
    for step in range(1, reach[0] + 1):
        for way, peer, sign in streams:
            if step > reach[way]:
                continue
            slot = lax.rem(me + n + sign * (step - 1), n)
            for a in range(k):
                for i in range(pieces):
                    if step > 1:
                        link(a, way, step - 1, slot, peer, i).wait_recv()
                    copy = link(a, way, step, slot, peer, i)
                    copy.start()
                    started.append(copy)
    for way, peer, sign in streams:
        last = reach[way]
        slot = lax.rem(me + n + sign * last, n)
        for a in range(k):
            for i in range(pieces):
                link(a, way, last, slot, peer, i).wait_recv()
    for copy in started:
        copy.wait_send()


def ring_gather(arrays, n, tag, pieces=4):
    outs = tuple(jax.ShapeDtypeStruct((n,) + x.shape[1:], x.dtype) for x in arrays)
    moved = sum(x.size * x.dtype.itemsize for x in outs)
    vmem = pl.BlockSpec(memory_space=pltpu.VMEM)
    k = len(arrays)
    return pl.pallas_call(
        functools.partial(_ring_kernel, n, k, pieces),
        out_shape=outs,
        in_specs=[vmem] * k,
        out_specs=tuple([vmem] * k),
        scratch_shapes=[
            pltpu.SemaphoreType.DMA((k, 2, n // 2 + 1, pieces)),
            pltpu.SemaphoreType.DMA((k, 2, n // 2 + 1, pieces)),
            pltpu.SemaphoreType.DMA((k,)),
        ],
        compiler_params=pltpu.CompilerParams(collective_id=tag, has_side_effects=True),
        cost_estimate=pl.CostEstimate(flops=0, transcendentals=0, bytes_accessed=2 * moved),
    )(*arrays)


def per_device(
    tokens, value_weight, down_panels, up_panels, cotangent, block_adapter, adapter_slot
):
    n_owners = lax.axis_size("dp")
    myself = lax.axis_index("dp")
    n_split = lax.axis_size("mp")
    my_part = lax.axis_index("mp")
    rows, width_dev = tokens.shape
    own_rows, kv_full = cotangent.shape
    kv_part = kv_full // n_split
    stored = down_panels.shape[0]
    blocks = rows // BLOCK_ROWS
    hits = block_adapter[:, None] == jnp.arange(adapter_slot.shape[0], dtype=jnp.int32)[None, :]
    slots_all = jnp.sum(jnp.where(hits, adapter_slot[None, :], 0), axis=1)
    owner_all = (slots_all // stored).reshape(n_owners, blocks)
    local_all = (slots_all % stored).reshape(n_owners, blocks)
    mine = owner_all == myself
    wanted = jnp.sum(jnp.where(mine, local_all, 0), axis=1)
    served = jnp.any(mine, axis=1)
    pick_mask = (wanted[:, None] == jnp.arange(stored, dtype=jnp.int32)[None, :]) & served[:, None]
    my_owner = lax.dynamic_index_in_dim(owner_all, myself, 0, keepdims=False)
    select_mask = my_owner[:, None] == jnp.arange(n_owners, dtype=jnp.int32)[None, :]

    up_cols = lax.dynamic_slice_in_dim(up_panels, my_part * kv_part, kv_part, 2)
    both = jnp.concatenate([down_panels, up_cols], axis=1)
    got = lax.all_to_all(jnp.take(both, wanted, axis=0), "dp", split_axis=0, concat_axis=0, tiled=True)
    mine_got = jnp.take(got, my_owner, axis=0)
    panel_a = mine_got[:, :width_dev]
    panel_b_cols = mine_got[:, width_dev:]
    early = own_rows // 2
    (cot_early,) = ring_gather([cotangent[None, :early]], n_split, 0, pieces=2)

    token_blocks = tokens.reshape(blocks, BLOCK_ROWS, width_dev)
    partial_value = jnp.dot(tokens, value_weight, preferred_element_type=jnp.float32)
    base = lax.psum_scatter(partial_value, "mp", scatter_dimension=0, tiled=True)
    down_part = jnp.einsum(
        "bnd,bdk->bnk", token_blocks, panel_a, preferred_element_type=jnp.float32
    ).astype(jnp.bfloat16)
    down_rows = down_part.size // kv_full
    up_rows = panel_b_cols.size // kv_full
    packed = jnp.concatenate(
        [
            down_part.reshape(down_rows, kv_full),
            panel_b_cols.reshape(up_rows, kv_full),
            cotangent[early:],
        ],
        axis=0,
    )
    (parts,) = ring_gather([packed[None]], n_split, 1, pieces=8)
    cot_all = jnp.concatenate([cot_early, parts[:, down_rows + up_rows:]], axis=1)
    cot_all = cot_all.reshape(rows, kv_full)
    cot_blocks = cot_all.reshape(blocks, BLOCK_ROWS, kv_full)
    down = jnp.sum(parts[:, :down_rows].astype(jnp.float32), axis=0)
    down = down.astype(jnp.bfloat16).reshape(blocks, BLOCK_ROWS, RANK)
    parts_up = parts[:, down_rows:down_rows + up_rows].reshape(n_split, blocks, RANK, kv_part)
    panel_b = parts_up.transpose(1, 2, 0, 3).reshape(blocks, RANK, kv_full)
    back = jnp.einsum(
        "bnc,bkc->bnk", cot_blocks, panel_b, preferred_element_type=jnp.float32
    ).astype(jnp.bfloat16)

    first_row = my_part * own_rows
    my_down = lax.dynamic_slice_in_dim(down.reshape(rows, RANK), first_row, own_rows, 0)
    my_up = lax.dynamic_index_in_dim(panel_b, first_row // BLOCK_ROWS, 0, keepdims=False)
    lifted = jnp.dot(my_down, my_up, preferred_element_type=jnp.float32)
    projected = (base + lifted).astype(jnp.bfloat16)

    select_bf = select_mask.astype(jnp.bfloat16)
    pick_bf = pick_mask.astype(jnp.bfloat16)
    cot_share = lax.dynamic_slice_in_dim(cot_blocks, my_part * kv_part, kv_part, 2)
    block_grad_b = jnp.einsum(
        "bnk,bnc->bkc", down, cot_share, preferred_element_type=jnp.float32
    )
    send_gb = jnp.einsum(
        "bo,bkc->okc", select_mask.astype(jnp.float32), block_grad_b,
        precision=lax.Precision.HIGHEST,
    )
    recv_gb = lax.all_to_all(send_gb, "dp", split_axis=0, concat_axis=0, tiled=True)
    grad_share = jnp.einsum(
        "ra,rkc->akc", pick_mask.astype(jnp.float32), recv_gb, precision=lax.Precision.HIGHEST
    ).astype(jnp.bfloat16)

    block_grad_a = jnp.einsum(
        "bnd,bnk->bdk", token_blocks, back, preferred_element_type=jnp.float32
    ).astype(jnp.bfloat16)
    send_ga = jnp.einsum(
        "bo,bdk->odk", select_bf, block_grad_a, preferred_element_type=jnp.float32
    ).astype(jnp.bfloat16)
    recv_ga = lax.all_to_all(send_ga, "dp", split_axis=0, concat_axis=0, tiled=True)
    grad_down = jnp.einsum(
        "ra,rdk->adk", pick_bf, recv_ga, preferred_element_type=jnp.float32
    ).astype(jnp.bfloat16)
    (shares,) = ring_gather([grad_share.reshape(1, -1, kv_full)], n_split, 2, pieces=2)
    shares = shares.reshape(n_split, stored, RANK, kv_part)
    grad_up = shares.transpose(1, 2, 0, 3).reshape(stored, RANK, kv_full)

    grad_base = jnp.einsum("nc,dc->nd", cot_all, value_weight, preferred_element_type=jnp.float32)
    through = jnp.einsum("bnk,bdk->bnd", back, panel_a, preferred_element_type=jnp.float32)
    grad_tokens = (grad_base + through.reshape(rows, width_dev)).astype(jnp.bfloat16)
    return (projected, grad_tokens, grad_down, grad_up)


def solution(mesh):
    placed = (
        P("dp", "mp"),
        P("mp", None),
        P("dp", "mp", None),
        P("dp", None, None),
        P(("dp", "mp"), None),
        P(),
        P(),
    )
    return jax.shard_map(
        per_device,
        mesh=mesh,
        in_specs=placed,
        out_specs=(P(("dp", "mp"), None), P("dp", "mp"), P("dp", "mp", None), P("dp", None, None)),
        check_vma=False,
    )
```

```python
import functools

import jax
import jax.numpy as jnp
from jax import lax
from jax.experimental import pallas as pl
from jax.experimental.pallas import tpu as pltpu
from jax.sharding import PartitionSpec as P

RANK = 64
BLOCK_ROWS = 128


def _ring_kernel(n, k, pieces, *refs):
    ins, outs = refs[:k], refs[k:2 * k]
    send_sems, recv_sems, local_sem = refs[2 * k:]
    me = lax.axis_index("mp")
    row = lax.axis_index("dp")
    right = lax.rem(me + 1, n)
    left = lax.rem(me + n - 1, n)
    barrier = pltpu.get_barrier_semaphore()
    for peer in (left, right):
        pl.semaphore_signal(
            barrier, inc=1, device_id=(row, peer), device_id_type=pl.DeviceIdType.MESH
        )
    pl.semaphore_wait(barrier, 2)
    for a in range(k):
        local = pltpu.make_async_copy(ins[a].at[0], outs[a].at[me], local_sem.at[a])
        local.start()
        local.wait()
    reach = (n // 2, n - 1 - n // 2)
    streams = ((0, right, -1), (1, left, 1))

    def link(a, way, step, slot, peer, i):
        size = outs[a].shape[1] // pieces
        part = outs[a].at[slot, pl.ds(i * size, size)]
        return pltpu.make_async_remote_copy(
            src_ref=part,
            dst_ref=part,
            send_sem=send_sems.at[a, way, step, i],
            recv_sem=recv_sems.at[a, way, step, i],
            device_id=(row, peer),
            device_id_type=pl.DeviceIdType.MESH,
        )

    started = []
    for step in range(1, reach[0] + 1):
        for way, peer, sign in streams:
            if step > reach[way]:
                continue
            slot = lax.rem(me + n + sign * (step - 1), n)
            for a in range(k):
                for i in range(pieces):
                    if step > 1:
                        link(a, way, step - 1, slot, peer, i).wait_recv()
                    copy = link(a, way, step, slot, peer, i)
                    copy.start()
                    started.append(copy)
    for way, peer, sign in streams:
        last = reach[way]
        slot = lax.rem(me + n + sign * last, n)
        for a in range(k):
            for i in range(pieces):
                link(a, way, last, slot, peer, i).wait_recv()
    for copy in started:
        copy.wait_send()


def ring_gather(arrays, n, tag, pieces=4):
    outs = tuple(jax.ShapeDtypeStruct((n,) + x.shape[1:], x.dtype) for x in arrays)
    moved = sum(x.size * x.dtype.itemsize for x in outs)
    vmem = pl.BlockSpec(memory_space=pltpu.VMEM)
    k = len(arrays)
    return pl.pallas_call(
        functools.partial(_ring_kernel, n, k, pieces),
        out_shape=outs,
        in_specs=[vmem] * k,
        out_specs=tuple([vmem] * k),
        scratch_shapes=[
            pltpu.SemaphoreType.DMA((k, 2, n // 2 + 1, pieces)),
            pltpu.SemaphoreType.DMA((k, 2, n // 2 + 1, pieces)),
            pltpu.SemaphoreType.DMA((k,)),
        ],
        compiler_params=pltpu.CompilerParams(collective_id=tag, has_side_effects=True),
        cost_estimate=pl.CostEstimate(flops=0, transcendentals=0, bytes_accessed=2 * moved),
    )(*arrays)


def per_device(
    tokens, value_weight, down_panels, up_panels, cotangent, block_adapter, adapter_slot
):
    n_owners = lax.axis_size("dp")
    myself = lax.axis_index("dp")
    n_split = lax.axis_size("mp")
    my_part = lax.axis_index("mp")
    rows, width_dev = tokens.shape
    own_rows, kv_full = cotangent.shape
    kv_part = kv_full // n_split
    stored = down_panels.shape[0]
    blocks = rows // BLOCK_ROWS
    hits = block_adapter[:, None] == jnp.arange(adapter_slot.shape[0], dtype=jnp.int32)[None, :]
    slots_all = jnp.sum(jnp.where(hits, adapter_slot[None, :], 0), axis=1)
    owner_all = (slots_all // stored).reshape(n_owners, blocks)
    local_all = (slots_all % stored).reshape(n_owners, blocks)
    mine = owner_all == myself
    wanted = jnp.sum(jnp.where(mine, local_all, 0), axis=1)
    served = jnp.any(mine, axis=1)
    pick_mask = (wanted[:, None] == jnp.arange(stored, dtype=jnp.int32)[None, :]) & served[:, None]
    my_owner = lax.dynamic_index_in_dim(owner_all, myself, 0, keepdims=False)
    select_mask = my_owner[:, None] == jnp.arange(n_owners, dtype=jnp.int32)[None, :]

    share = RANK // n_split
    up_rows_mine = lax.dynamic_slice_in_dim(up_panels, my_part * share, share, 1)
    both = jnp.concatenate([down_panels, up_rows_mine.reshape(stored, -1, RANK)], axis=1)
    got = lax.all_to_all(jnp.take(both, wanted, axis=0), "dp", split_axis=0, concat_axis=0, tiled=True)
    mine_got = jnp.take(got, my_owner, axis=0)
    panel_a = mine_got[:, :width_dev]
    panel_b_cols = mine_got[:, width_dev:]
    (cot_all,) = ring_gather([cotangent[None]], n_split, 0)
    cot_all = cot_all.reshape(rows, kv_full)
    cot_blocks = cot_all.reshape(blocks, BLOCK_ROWS, kv_full)

    token_blocks = tokens.reshape(blocks, BLOCK_ROWS, width_dev)
    partial_value = jnp.dot(tokens, value_weight, preferred_element_type=jnp.float32)
    base = lax.psum_scatter(partial_value, "mp", scatter_dimension=0, tiled=True)
    down_part = jnp.einsum(
        "bnd,bdk->bnk", token_blocks, panel_a, preferred_element_type=jnp.float32
    ).astype(jnp.bfloat16)
    down_rows = down_part.size // kv_full
    packed = jnp.concatenate(
        [down_part.reshape(down_rows, kv_full), panel_b_cols.reshape(-1, kv_full)], axis=0
    )
    (parts,) = ring_gather([packed[None]], n_split, 1, pieces=3)
    down = jnp.sum(parts[:, :down_rows].astype(jnp.float32), axis=0)
    down = down.astype(jnp.bfloat16).reshape(blocks, BLOCK_ROWS, RANK)
    parts_up = parts[:, down_rows:].reshape(n_split, blocks, share, kv_full)
    back = jnp.einsum(
        "bnc,jbqc->bnjq", cot_blocks, parts_up, preferred_element_type=jnp.float32
    ).reshape(blocks, BLOCK_ROWS, RANK).astype(jnp.bfloat16)

    first_row = my_part * own_rows
    my_down = lax.dynamic_slice_in_dim(down.reshape(rows, RANK), first_row, own_rows, 0)
    my_up = lax.dynamic_index_in_dim(parts_up, first_row // BLOCK_ROWS, 1, keepdims=False)
    my_up = my_up.reshape(RANK, kv_full)
    lifted = jnp.dot(my_down, my_up, preferred_element_type=jnp.float32)
    projected = (base + lifted).astype(jnp.bfloat16)

    select_bf = select_mask.astype(jnp.bfloat16)
    pick_bf = pick_mask.astype(jnp.bfloat16)
    down_share = lax.dynamic_slice_in_dim(down, my_part * share, share, 2)
    block_grad_b = jnp.einsum(
        "bnq,bnc->bqc", down_share, cot_blocks, preferred_element_type=jnp.float32
    )
    send_gb = jnp.einsum(
        "bo,bkc->okc", select_mask.astype(jnp.float32), block_grad_b,
        precision=lax.Precision.HIGHEST,
    )
    recv_gb = lax.all_to_all(send_gb, "dp", split_axis=0, concat_axis=0, tiled=True)
    grad_share = jnp.einsum(
        "ra,rkc->akc", pick_mask.astype(jnp.float32), recv_gb, precision=lax.Precision.HIGHEST
    ).astype(jnp.bfloat16)

    block_grad_a = jnp.einsum(
        "bnd,bnk->bdk", token_blocks, back, preferred_element_type=jnp.float32
    ).astype(jnp.bfloat16)
    send_ga = jnp.einsum(
        "bo,bdk->odk", select_bf, block_grad_a, preferred_element_type=jnp.float32
    ).astype(jnp.bfloat16)
    recv_ga = lax.all_to_all(send_ga, "dp", split_axis=0, concat_axis=0, tiled=True)
    grad_down = jnp.einsum(
        "ra,rdk->adk", pick_bf, recv_ga, preferred_element_type=jnp.float32
    ).astype(jnp.bfloat16)
    (shares,) = ring_gather([grad_share.reshape(1, -1, kv_full)], n_split, 2, pieces=2)
    shares = shares.reshape(n_split, stored, share, kv_full)
    grad_up = shares.transpose(1, 0, 2, 3).reshape(stored, RANK, kv_full)

    grad_base = jnp.einsum("nc,dc->nd", cot_all, value_weight, preferred_element_type=jnp.float32)
    through = jnp.einsum("bnk,bdk->bnd", back, panel_a, preferred_element_type=jnp.float32)
    grad_tokens = (grad_base + through.reshape(rows, width_dev)).astype(jnp.bfloat16)
    return (projected, grad_tokens, grad_down, grad_up)


def solution(mesh):
    placed = (
        P("dp", "mp"),
        P("mp", None),
        P("dp", "mp", None),
        P("dp", None, None),
        P(("dp", "mp"), None),
        P(),
        P(),
    )
    return jax.shard_map(
        per_device,
        mesh=mesh,
        in_specs=placed,
        out_specs=(P(("dp", "mp"), None), P("dp", "mp"), P("dp", "mp", None), P("dp", None, None)),
        check_vma=False,
    )
```

```python
import functools

import jax
import jax.numpy as jnp
from jax import lax
from jax.experimental import pallas as pl
from jax.experimental.pallas import tpu as pltpu
from jax.sharding import PartitionSpec as P

RANK = 64
BLOCK_ROWS = 128


def _ring_kernel(n, k, pieces, *refs):
    ins, outs = refs[:k], refs[k:2 * k]
    send_sems, recv_sems, local_sem = refs[2 * k:]
    me = lax.axis_index("mp")
    row = lax.axis_index("dp")
    right = lax.rem(me + 1, n)
    left = lax.rem(me + n - 1, n)
    barrier = pltpu.get_barrier_semaphore()
    for peer in (left, right):
        pl.semaphore_signal(
            barrier, inc=1, device_id=(row, peer), device_id_type=pl.DeviceIdType.MESH
        )
    pl.semaphore_wait(barrier, 2)
    for a in range(k):
        local = pltpu.make_async_copy(ins[a].at[0], outs[a].at[me], local_sem.at[a])
        local.start()
        local.wait()
    reach = (n // 2, n - 1 - n // 2)
    streams = ((0, right, -1), (1, left, 1))

    def link(a, way, step, slot, peer, i):
        size = outs[a].shape[1] // pieces
        part = outs[a].at[slot, pl.ds(i * size, size)]
        return pltpu.make_async_remote_copy(
            src_ref=part,
            dst_ref=part,
            send_sem=send_sems.at[a, way, step, i],
            recv_sem=recv_sems.at[a, way, step, i],
            device_id=(row, peer),
            device_id_type=pl.DeviceIdType.MESH,
        )

    started = []
    for step in range(1, reach[0] + 1):
        for way, peer, sign in streams:
            if step > reach[way]:
                continue
            slot = lax.rem(me + n + sign * (step - 1), n)
            for a in range(k):
                for i in range(pieces):
                    if step > 1:
                        link(a, way, step - 1, slot, peer, i).wait_recv()
                    copy = link(a, way, step, slot, peer, i)
                    copy.start()
                    started.append(copy)
    for way, peer, sign in streams:
        last = reach[way]
        slot = lax.rem(me + n + sign * last, n)
        for a in range(k):
            for i in range(pieces):
                link(a, way, last, slot, peer, i).wait_recv()
    for copy in started:
        copy.wait_send()


def ring_gather(arrays, n, tag, pieces=4):
    outs = tuple(jax.ShapeDtypeStruct((n,) + x.shape[1:], x.dtype) for x in arrays)
    moved = sum(x.size * x.dtype.itemsize for x in outs)
    vmem = pl.BlockSpec(memory_space=pltpu.VMEM)
    k = len(arrays)
    return pl.pallas_call(
        functools.partial(_ring_kernel, n, k, pieces),
        out_shape=outs,
        in_specs=[vmem] * k,
        out_specs=tuple([vmem] * k),
        scratch_shapes=[
            pltpu.SemaphoreType.DMA((k, 2, n // 2 + 1, pieces)),
            pltpu.SemaphoreType.DMA((k, 2, n // 2 + 1, pieces)),
            pltpu.SemaphoreType.DMA((k,)),
        ],
        compiler_params=pltpu.CompilerParams(collective_id=tag, has_side_effects=True),
        cost_estimate=pl.CostEstimate(flops=0, transcendentals=0, bytes_accessed=2 * moved),
    )(*arrays)


def per_device(
    tokens, value_weight, down_panels, up_panels, cotangent, block_adapter, adapter_slot
):
    n_owners = lax.axis_size("dp")
    myself = lax.axis_index("dp")
    n_split = lax.axis_size("mp")
    my_part = lax.axis_index("mp")
    rows, width_dev = tokens.shape
    own_rows, kv_full = cotangent.shape
    kv_part = kv_full // n_split
    stored = down_panels.shape[0]
    blocks = rows // BLOCK_ROWS
    hits = block_adapter[:, None] == jnp.arange(adapter_slot.shape[0], dtype=jnp.int32)[None, :]
    slots_all = jnp.sum(jnp.where(hits, adapter_slot[None, :], 0), axis=1)
    owner_all = (slots_all // stored).reshape(n_owners, blocks)
    local_all = (slots_all % stored).reshape(n_owners, blocks)
    mine = owner_all == myself
    wanted = jnp.sum(jnp.where(mine, local_all, 0), axis=1)
    served = jnp.any(mine, axis=1)
    pick_mask = (wanted[:, None] == jnp.arange(stored, dtype=jnp.int32)[None, :]) & served[:, None]
    my_owner = lax.dynamic_index_in_dim(owner_all, myself, 0, keepdims=False)
    select_mask = my_owner[:, None] == jnp.arange(n_owners, dtype=jnp.int32)[None, :]

    share = RANK // n_split
    up_rows_mine = lax.dynamic_slice_in_dim(up_panels, my_part * share, share, 1)
    both = jnp.concatenate([down_panels, up_rows_mine.reshape(stored, -1, RANK)], axis=1)
    got = lax.all_to_all(jnp.take(both, wanted, axis=0), "dp", split_axis=0, concat_axis=0, tiled=True)

    (cot_all,) = ring_gather([cotangent[None]], n_split, 0)
    got, cot_all = lax.optimization_barrier((got, cot_all))
    mine_got = jnp.take(got, my_owner, axis=0)
    panel_a = mine_got[:, :width_dev]
    panel_b_cols = mine_got[:, width_dev:]
    cot_all = cot_all.reshape(rows, kv_full)
    cot_blocks = cot_all.reshape(blocks, BLOCK_ROWS, kv_full)

    token_blocks = tokens.reshape(blocks, BLOCK_ROWS, width_dev)
    partial_value = jnp.dot(tokens, value_weight, preferred_element_type=jnp.float32)
    down_part = jnp.einsum(
        "bnd,bdk->bnk", token_blocks, panel_a, preferred_element_type=jnp.float32
    ).astype(jnp.bfloat16)
    down_rows = down_part.size // kv_full
    packed = jnp.concatenate(
        [down_part.reshape(down_rows, kv_full), panel_b_cols.reshape(-1, kv_full)], axis=0
    )
    (parts,) = ring_gather([packed[None]], n_split, 1, pieces=3)
    partial_value, parts = lax.optimization_barrier((partial_value, parts))
    base = lax.psum_scatter(partial_value, "mp", scatter_dimension=0, tiled=True)
    down = jnp.sum(parts[:, :down_rows].astype(jnp.float32), axis=0)
    down = down.astype(jnp.bfloat16).reshape(blocks, BLOCK_ROWS, RANK)
    parts_up = parts[:, down_rows:].reshape(n_split, blocks, share, kv_full)
    back = jnp.einsum(
        "bnc,jbqc->bnjq", cot_blocks, parts_up, preferred_element_type=jnp.float32
    ).reshape(blocks, BLOCK_ROWS, RANK).astype(jnp.bfloat16)

    first_row = my_part * own_rows
    my_down = lax.dynamic_slice_in_dim(down.reshape(rows, RANK), first_row, own_rows, 0)
    my_up = lax.dynamic_index_in_dim(parts_up, first_row // BLOCK_ROWS, 1, keepdims=False)
    my_up = my_up.reshape(RANK, kv_full)
    lifted = jnp.dot(my_down, my_up, preferred_element_type=jnp.float32)
    projected = (base + lifted).astype(jnp.bfloat16)

    select_bf = select_mask.astype(jnp.bfloat16)
    pick_bf = pick_mask.astype(jnp.bfloat16)
    down_share = lax.dynamic_slice_in_dim(down, my_part * share, share, 2)
    block_grad_b = jnp.einsum(
        "bnq,bnc->bqc", down_share, cot_blocks, preferred_element_type=jnp.float32
    )
    send_gb = jnp.einsum(
        "bo,bkc->okc", select_mask.astype(jnp.float32), block_grad_b,
        precision=lax.Precision.HIGHEST,
    )
    recv_gb = lax.all_to_all(send_gb, "dp", split_axis=0, concat_axis=0, tiled=True)
    grad_share = jnp.einsum(
        "ra,rkc->akc", pick_mask.astype(jnp.float32), recv_gb, precision=lax.Precision.HIGHEST
    ).astype(jnp.bfloat16)

    block_grad_a = jnp.einsum(
        "bnd,bnk->bdk", token_blocks, back, preferred_element_type=jnp.float32
    ).astype(jnp.bfloat16)
    send_ga = jnp.einsum(
        "bo,bdk->odk", select_bf, block_grad_a, preferred_element_type=jnp.float32
    ).astype(jnp.bfloat16)
    recv_ga = lax.all_to_all(send_ga, "dp", split_axis=0, concat_axis=0, tiled=True)
    grad_down = jnp.einsum(
        "ra,rdk->adk", pick_bf, recv_ga, preferred_element_type=jnp.float32
    ).astype(jnp.bfloat16)
    (shares,) = ring_gather([grad_share.reshape(1, -1, kv_full)], n_split, 2, pieces=2)
    shares = shares.reshape(n_split, stored, share, kv_full)
    grad_up = shares.transpose(1, 0, 2, 3).reshape(stored, RANK, kv_full)

    grad_base = jnp.einsum("nc,dc->nd", cot_all, value_weight, preferred_element_type=jnp.float32)
    through = jnp.einsum("bnk,bdk->bnd", back, panel_a, preferred_element_type=jnp.float32)
    grad_tokens = (grad_base + through.reshape(rows, width_dev)).astype(jnp.bfloat16)
    return (projected, grad_tokens, grad_down, grad_up)


def solution(mesh):
    placed = (
        P("dp", "mp"),
        P("mp", None),
        P("dp", "mp", None),
        P("dp", None, None),
        P(("dp", "mp"), None),
        P(),
        P(),
    )
    return jax.shard_map(
        per_device,
        mesh=mesh,
        in_specs=placed,
        out_specs=(P(("dp", "mp"), None), P("dp", "mp"), P("dp", "mp", None), P("dp", None, None)),
        check_vma=False,
    )
```

```python
import functools

import jax
import jax.numpy as jnp
from jax import lax
from jax.experimental import pallas as pl
from jax.experimental.pallas import tpu as pltpu
from jax.sharding import PartitionSpec as P

RANK = 64
BLOCK_ROWS = 128


def _ring_kernel(n, k, pieces, *refs):
    ins, outs = refs[:k], refs[k:2 * k]
    send_sems, recv_sems, local_sem = refs[2 * k:]
    me = lax.axis_index("mp")
    row = lax.axis_index("dp")
    right = lax.rem(me + 1, n)
    left = lax.rem(me + n - 1, n)
    barrier = pltpu.get_barrier_semaphore()
    for peer in (left, right):
        pl.semaphore_signal(
            barrier, inc=1, device_id=(row, peer), device_id_type=pl.DeviceIdType.MESH
        )
    pl.semaphore_wait(barrier, 2)
    for a in range(k):
        local = pltpu.make_async_copy(ins[a].at[0], outs[a].at[me], local_sem.at[a])
        local.start()
        local.wait()
    reach = (n // 2, n - 1 - n // 2)
    streams = ((0, right, -1), (1, left, 1))

    def link(a, way, step, slot, peer, i):
        size = outs[a].shape[1] // pieces
        part = outs[a].at[slot, pl.ds(i * size, size)]
        return pltpu.make_async_remote_copy(
            src_ref=part,
            dst_ref=part,
            send_sem=send_sems.at[a, way, step, i],
            recv_sem=recv_sems.at[a, way, step, i],
            device_id=(row, peer),
            device_id_type=pl.DeviceIdType.MESH,
        )

    started = []
    for step in range(1, reach[0] + 1):
        for way, peer, sign in streams:
            if step > reach[way]:
                continue
            slot = lax.rem(me + n + sign * (step - 1), n)
            for a in range(k):
                for i in range(pieces):
                    if step > 1:
                        link(a, way, step - 1, slot, peer, i).wait_recv()
                    copy = link(a, way, step, slot, peer, i)
                    copy.start()
                    started.append(copy)
    for way, peer, sign in streams:
        last = reach[way]
        slot = lax.rem(me + n + sign * last, n)
        for a in range(k):
            for i in range(pieces):
                link(a, way, last, slot, peer, i).wait_recv()
    for copy in started:
        copy.wait_send()


def ring_gather(arrays, n, tag, pieces=4):
    outs = tuple(jax.ShapeDtypeStruct((n,) + x.shape[1:], x.dtype) for x in arrays)
    moved = sum(x.size * x.dtype.itemsize for x in outs)
    vmem = pl.BlockSpec(memory_space=pltpu.VMEM)
    k = len(arrays)
    return pl.pallas_call(
        functools.partial(_ring_kernel, n, k, pieces),
        out_shape=outs,
        in_specs=[vmem] * k,
        out_specs=tuple([vmem] * k),
        scratch_shapes=[
            pltpu.SemaphoreType.DMA((k, 2, n // 2 + 1, pieces)),
            pltpu.SemaphoreType.DMA((k, 2, n // 2 + 1, pieces)),
            pltpu.SemaphoreType.DMA((k,)),
        ],
        compiler_params=pltpu.CompilerParams(collective_id=tag, has_side_effects=True),
        cost_estimate=pl.CostEstimate(flops=0, transcendentals=0, bytes_accessed=2 * moved),
    )(*arrays)


def per_device(
    tokens, value_weight, down_panels, up_panels, cotangent, block_adapter, adapter_slot
):
    n_owners = lax.axis_size("dp")
    myself = lax.axis_index("dp")
    n_split = lax.axis_size("mp")
    my_part = lax.axis_index("mp")
    rows, width_dev = tokens.shape
    own_rows, kv_full = cotangent.shape
    kv_part = kv_full // n_split
    stored = down_panels.shape[0]
    blocks = rows // BLOCK_ROWS
    hits = block_adapter[:, None] == jnp.arange(adapter_slot.shape[0], dtype=jnp.int32)[None, :]
    slots_all = jnp.sum(jnp.where(hits, adapter_slot[None, :], 0), axis=1)
    owner_all = (slots_all // stored).reshape(n_owners, blocks)
    local_all = (slots_all % stored).reshape(n_owners, blocks)
    mine = owner_all == myself
    wanted = jnp.sum(jnp.where(mine, local_all, 0), axis=1)
    served = jnp.any(mine, axis=1)
    pick_mask = (wanted[:, None] == jnp.arange(stored, dtype=jnp.int32)[None, :]) & served[:, None]
    my_owner = lax.dynamic_index_in_dim(owner_all, myself, 0, keepdims=False)
    select_mask = my_owner[:, None] == jnp.arange(n_owners, dtype=jnp.int32)[None, :]

    share = RANK // n_split
    up_rows_mine = lax.dynamic_slice_in_dim(up_panels, my_part * share, share, 1)
    both = jnp.concatenate([down_panels, up_rows_mine.reshape(stored, -1, RANK)], axis=1)
    got = lax.all_to_all(jnp.take(both, wanted, axis=0), "dp", split_axis=0, concat_axis=0, tiled=True)

    (cot_all,) = ring_gather([cotangent[None]], n_split, 0)
    got, cot_all = lax.optimization_barrier((got, cot_all))
    mine_got = jnp.take(got, my_owner, axis=0)
    panel_a = mine_got[:, :width_dev]
    panel_b_cols = mine_got[:, width_dev:]
    cot_all = cot_all.reshape(rows, kv_full)
    cot_blocks = cot_all.reshape(blocks, BLOCK_ROWS, kv_full)

    token_blocks = tokens.reshape(blocks, BLOCK_ROWS, width_dev)
    partial_value = jnp.dot(tokens, value_weight, preferred_element_type=jnp.float32)
    down_part = jnp.einsum(
        "bnd,bdk->bnk", token_blocks, panel_a, preferred_element_type=jnp.float32
    ).astype(jnp.bfloat16)
    down_rows = down_part.size // kv_full
    packed = jnp.concatenate(
        [down_part.reshape(down_rows, kv_full), panel_b_cols.reshape(-1, kv_full)], axis=0
    )
    (parts,) = ring_gather([packed[None]], n_split, 1, pieces=3)
    partial_value, parts = lax.optimization_barrier((partial_value, parts))
    base = lax.psum_scatter(partial_value, "mp", scatter_dimension=0, tiled=True)
    down = jnp.sum(parts[:, :down_rows].astype(jnp.float32), axis=0)
    down = down.astype(jnp.bfloat16).reshape(blocks, BLOCK_ROWS, RANK)
    parts_up = parts[:, down_rows:].reshape(n_split, blocks, share, kv_full)
    back = jnp.einsum(
        "bnc,jbqc->bnjq", cot_blocks, parts_up, preferred_element_type=jnp.float32
    ).reshape(blocks, BLOCK_ROWS, RANK).astype(jnp.bfloat16)

    first_row = my_part * own_rows
    my_down = lax.dynamic_slice_in_dim(down.reshape(rows, RANK), first_row, own_rows, 0)
    my_up = lax.dynamic_index_in_dim(parts_up, first_row // BLOCK_ROWS, 1, keepdims=False)
    my_up = my_up.reshape(RANK, kv_full)
    lifted = jnp.dot(my_down, my_up, preferred_element_type=jnp.float32)
    projected = (base + lifted).astype(jnp.bfloat16)

    select_bf = select_mask.astype(jnp.bfloat16)
    pick_bf = pick_mask.astype(jnp.bfloat16)
    down_share = lax.dynamic_slice_in_dim(down, my_part * share, share, 2)
    block_grad_b = jnp.einsum(
        "bnq,bnc->bqc", down_share, cot_blocks, preferred_element_type=jnp.float32
    )
    send_gb = jnp.sum(
        jnp.where(select_mask[:, :, None, None], block_grad_b[:, None], 0.0), axis=0
    )
    recv_gb = lax.all_to_all(send_gb, "dp", split_axis=0, concat_axis=0, tiled=True)
    grad_share = jnp.sum(
        jnp.where(pick_mask[:, :, None, None], recv_gb[:, None], 0.0), axis=0
    ).astype(jnp.bfloat16)

    block_grad_a = jnp.einsum(
        "bnd,bnk->bdk", token_blocks, back, preferred_element_type=jnp.float32
    ).astype(jnp.bfloat16)
    send_ga = jnp.einsum(
        "bo,bdk->odk", select_bf, block_grad_a, preferred_element_type=jnp.float32
    ).astype(jnp.bfloat16)
    recv_ga = lax.all_to_all(send_ga, "dp", split_axis=0, concat_axis=0, tiled=True)
    grad_down = jnp.einsum(
        "ra,rdk->adk", pick_bf, recv_ga, preferred_element_type=jnp.float32
    ).astype(jnp.bfloat16)
    (shares,) = ring_gather([grad_share.reshape(1, -1, kv_full)], n_split, 2, pieces=2)
    shares = shares.reshape(n_split, stored, share, kv_full)
    grad_up = shares.transpose(1, 0, 2, 3).reshape(stored, RANK, kv_full)

    grad_base = jnp.einsum("nc,dc->nd", cot_all, value_weight, preferred_element_type=jnp.float32)
    through = jnp.einsum("bnk,bdk->bnd", back, panel_a, preferred_element_type=jnp.float32)
    grad_tokens = (grad_base + through.reshape(rows, width_dev)).astype(jnp.bfloat16)
    return (projected, grad_tokens, grad_down, grad_up)


def solution(mesh):
    placed = (
        P("dp", "mp"),
        P("mp", None),
        P("dp", "mp", None),
        P("dp", None, None),
        P(("dp", "mp"), None),
        P(),
        P(),
    )
    return jax.shard_map(
        per_device,
        mesh=mesh,
        in_specs=placed,
        out_specs=(P(("dp", "mp"), None), P("dp", "mp"), P("dp", "mp", None), P("dp", None, None)),
        check_vma=False,
    )
```

```python
import functools

import jax
import jax.numpy as jnp
from jax import lax
from jax.experimental import pallas as pl
from jax.experimental.pallas import tpu as pltpu
from jax.sharding import PartitionSpec as P

RANK = 64
BLOCK_ROWS = 128


def _ring_kernel(n, k, pieces, *refs):
    ins, outs = refs[:k], refs[k:2 * k]
    send_sems, recv_sems, local_sem = refs[2 * k:]
    me = lax.axis_index("mp")
    row = lax.axis_index("dp")
    right = lax.rem(me + 1, n)
    left = lax.rem(me + n - 1, n)
    barrier = pltpu.get_barrier_semaphore()
    for peer in (left, right):
        pl.semaphore_signal(
            barrier, inc=1, device_id=(row, peer), device_id_type=pl.DeviceIdType.MESH
        )
    pl.semaphore_wait(barrier, 2)
    for a in range(k):
        local = pltpu.make_async_copy(ins[a].at[0], outs[a].at[me], local_sem.at[a])
        local.start()
        local.wait()
    reach = (n // 2, n - 1 - n // 2)
    streams = ((0, right, -1), (1, left, 1))

    def link(a, way, step, slot, peer, i):
        size = outs[a].shape[1] // pieces
        part = outs[a].at[slot, pl.ds(i * size, size)]
        return pltpu.make_async_remote_copy(
            src_ref=part,
            dst_ref=part,
            send_sem=send_sems.at[a, way, step, i],
            recv_sem=recv_sems.at[a, way, step, i],
            device_id=(row, peer),
            device_id_type=pl.DeviceIdType.MESH,
        )

    started = []
    for step in range(1, reach[0] + 1):
        for way, peer, sign in streams:
            if step > reach[way]:
                continue
            slot = lax.rem(me + n + sign * (step - 1), n)
            for a in range(k):
                for i in range(pieces):
                    if step > 1:
                        link(a, way, step - 1, slot, peer, i).wait_recv()
                    copy = link(a, way, step, slot, peer, i)
                    copy.start()
                    started.append(copy)
    for way, peer, sign in streams:
        last = reach[way]
        slot = lax.rem(me + n + sign * last, n)
        for a in range(k):
            for i in range(pieces):
                link(a, way, last, slot, peer, i).wait_recv()
    for copy in started:
        copy.wait_send()


def ring_gather(arrays, n, tag, pieces=4):
    outs = tuple(jax.ShapeDtypeStruct((n,) + x.shape[1:], x.dtype) for x in arrays)
    moved = sum(x.size * x.dtype.itemsize for x in outs)
    vmem = pl.BlockSpec(memory_space=pltpu.VMEM)
    k = len(arrays)
    return pl.pallas_call(
        functools.partial(_ring_kernel, n, k, pieces),
        out_shape=outs,
        in_specs=[vmem] * k,
        out_specs=tuple([vmem] * k),
        scratch_shapes=[
            pltpu.SemaphoreType.DMA((k, 2, n // 2 + 1, pieces)),
            pltpu.SemaphoreType.DMA((k, 2, n // 2 + 1, pieces)),
            pltpu.SemaphoreType.DMA((k,)),
        ],
        compiler_params=pltpu.CompilerParams(collective_id=tag, has_side_effects=True),
        cost_estimate=pl.CostEstimate(flops=0, transcendentals=0, bytes_accessed=2 * moved),
    )(*arrays)


def per_device(
    tokens, value_weight, down_panels, up_panels, cotangent, block_adapter, adapter_slot
):
    n_owners = lax.axis_size("dp")
    myself = lax.axis_index("dp")
    n_split = lax.axis_size("mp")
    my_part = lax.axis_index("mp")
    rows, width_dev = tokens.shape
    own_rows, kv_full = cotangent.shape
    kv_part = kv_full // n_split
    stored = down_panels.shape[0]
    blocks = rows // BLOCK_ROWS
    hits = block_adapter[:, None] == jnp.arange(adapter_slot.shape[0], dtype=jnp.int32)[None, :]
    slots_all = jnp.sum(jnp.where(hits, adapter_slot[None, :], 0), axis=1)
    owner_all = (slots_all // stored).reshape(n_owners, blocks)
    local_all = (slots_all % stored).reshape(n_owners, blocks)
    mine = owner_all == myself
    wanted = jnp.sum(jnp.where(mine, local_all, 0), axis=1)
    served = jnp.any(mine, axis=1)
    pick_mask = (wanted[:, None] == jnp.arange(stored, dtype=jnp.int32)[None, :]) & served[:, None]
    my_owner = lax.dynamic_index_in_dim(owner_all, myself, 0, keepdims=False)
    select_mask = my_owner[:, None] == jnp.arange(n_owners, dtype=jnp.int32)[None, :]

    share = RANK // n_split
    up_rows_mine = lax.dynamic_slice_in_dim(up_panels, my_part * share, share, 1)
    both = jnp.concatenate([down_panels, up_rows_mine.reshape(stored, -1, RANK)], axis=1)
    got = lax.all_to_all(jnp.take(both, wanted, axis=0), "dp", split_axis=0, concat_axis=0, tiled=True)

    (cot_all,) = ring_gather([cotangent[None]], n_split, 0)
    got, cot_all = lax.optimization_barrier((got, cot_all))
    mine_got = jnp.take(got, my_owner, axis=0)
    panel_a = mine_got[:, :width_dev]
    panel_b_cols = mine_got[:, width_dev:]
    cot_all = cot_all.reshape(rows, kv_full)
    cot_blocks = cot_all.reshape(blocks, BLOCK_ROWS, kv_full)

    token_blocks = tokens.reshape(blocks, BLOCK_ROWS, width_dev)
    partial_value = jnp.dot(tokens, value_weight, preferred_element_type=jnp.float32)
    down_part = jnp.einsum(
        "bnd,bdk->bnk", token_blocks, panel_a, preferred_element_type=jnp.float32
    ).astype(jnp.bfloat16)
    down_rows = down_part.size // kv_full
    packed = jnp.concatenate(
        [down_part.reshape(down_rows, kv_full), panel_b_cols.reshape(-1, kv_full)], axis=0
    )
    (parts,) = ring_gather([packed[None]], n_split, 1, pieces=6)
    partial_value, parts = lax.optimization_barrier((partial_value, parts))
    base = lax.psum_scatter(partial_value, "mp", scatter_dimension=0, tiled=True)
    down = jnp.sum(parts[:, :down_rows].astype(jnp.float32), axis=0)
    down = down.astype(jnp.bfloat16).reshape(blocks, BLOCK_ROWS, RANK)
    parts_up = parts[:, down_rows:].reshape(n_split, blocks, share, kv_full)
    back = jnp.einsum(
        "bnc,jbqc->bnjq", cot_blocks, parts_up, preferred_element_type=jnp.float32
    ).reshape(blocks, BLOCK_ROWS, RANK).astype(jnp.bfloat16)

    first_row = my_part * own_rows
    my_down = lax.dynamic_slice_in_dim(down.reshape(rows, RANK), first_row, own_rows, 0)
    my_up = lax.dynamic_index_in_dim(parts_up, first_row // BLOCK_ROWS, 1, keepdims=False)
    my_up = my_up.reshape(RANK, kv_full)
    lifted = jnp.dot(my_down, my_up, preferred_element_type=jnp.float32)
    projected = (base + lifted).astype(jnp.bfloat16)

    select_bf = select_mask.astype(jnp.bfloat16)
    pick_bf = pick_mask.astype(jnp.bfloat16)
    down_share = lax.dynamic_slice_in_dim(down, my_part * share, share, 2)
    block_grad_b = jnp.einsum(
        "bnq,bnc->bqc", down_share, cot_blocks, preferred_element_type=jnp.float32
    )
    send_gb = jnp.einsum(
        "bo,bkc->okc", select_mask.astype(jnp.float32), block_grad_b,
        precision=lax.Precision.HIGHEST,
    )
    recv_gb = lax.all_to_all(send_gb, "dp", split_axis=0, concat_axis=0, tiled=True)
    grad_share = jnp.einsum(
        "ra,rkc->akc", pick_mask.astype(jnp.float32), recv_gb, precision=lax.Precision.HIGHEST
    ).astype(jnp.bfloat16)

    block_grad_a = jnp.einsum(
        "bnd,bnk->bdk", token_blocks, back, preferred_element_type=jnp.float32
    ).astype(jnp.bfloat16)
    send_ga = jnp.einsum(
        "bo,bdk->odk", select_bf, block_grad_a, preferred_element_type=jnp.float32
    ).astype(jnp.bfloat16)
    recv_ga = lax.all_to_all(send_ga, "dp", split_axis=0, concat_axis=0, tiled=True)
    grad_down = jnp.einsum(
        "ra,rdk->adk", pick_bf, recv_ga, preferred_element_type=jnp.float32
    ).astype(jnp.bfloat16)
    (shares,) = ring_gather([grad_share.reshape(1, -1, kv_full)], n_split, 2, pieces=2)
    shares = shares.reshape(n_split, stored, share, kv_full)
    grad_up = shares.transpose(1, 0, 2, 3).reshape(stored, RANK, kv_full)

    grad_base = jnp.einsum("nc,dc->nd", cot_all, value_weight, preferred_element_type=jnp.float32)
    through = jnp.einsum("bnk,bdk->bnd", back, panel_a, preferred_element_type=jnp.float32)
    grad_tokens = (grad_base + through.reshape(rows, width_dev)).astype(jnp.bfloat16)
    return (projected, grad_tokens, grad_down, grad_up)


def solution(mesh):
    placed = (
        P("dp", "mp"),
        P("mp", None),
        P("dp", "mp", None),
        P("dp", None, None),
        P(("dp", "mp"), None),
        P(),
        P(),
    )
    return jax.shard_map(
        per_device,
        mesh=mesh,
        in_specs=placed,
        out_specs=(P(("dp", "mp"), None), P("dp", "mp"), P("dp", "mp", None), P("dp", None, None)),
        check_vma=False,
    )
```

```python
import functools

import jax
import jax.numpy as jnp
from jax import lax
from jax.experimental import pallas as pl
from jax.experimental.pallas import tpu as pltpu
from jax.sharding import PartitionSpec as P

RANK = 64
BLOCK_ROWS = 128


def _ring_kernel(n, k, pieces, *refs):
    ins, outs = refs[:k], refs[k:2 * k]
    send_sems, recv_sems, local_sem = refs[2 * k:]
    me = lax.axis_index("mp")
    row = lax.axis_index("dp")
    right = lax.rem(me + 1, n)
    left = lax.rem(me + n - 1, n)
    barrier = pltpu.get_barrier_semaphore()
    for peer in (left, right):
        pl.semaphore_signal(
            barrier, inc=1, device_id=(row, peer), device_id_type=pl.DeviceIdType.MESH
        )
    pl.semaphore_wait(barrier, 2)
    locals_ = []
    for a in range(k):
        local = pltpu.make_async_copy(ins[a].at[0], outs[a].at[me], local_sem.at[a])
        local.start()
        locals_.append(local)
    reach = (n // 2, n - 1 - n // 2)
    streams = ((0, right, -1), (1, left, 1))

    def link(a, way, step, slot, peer, i):
        size = outs[a].shape[1] // pieces
        part = outs[a].at[slot, pl.ds(i * size, size)]
        own = ins[a].at[0, pl.ds(i * size, size)]
        return pltpu.make_async_remote_copy(
            src_ref=own if step == 1 else part,
            dst_ref=part,
            send_sem=send_sems.at[a, way, step, i],
            recv_sem=recv_sems.at[a, way, step, i],
            device_id=(row, peer),
            device_id_type=pl.DeviceIdType.MESH,
        )

    started = []
    for step in range(1, reach[0] + 1):
        for way, peer, sign in streams:
            if step > reach[way]:
                continue
            slot = lax.rem(me + n + sign * (step - 1), n)
            for a in range(k):
                for i in range(pieces):
                    if step > 1:
                        link(a, way, step - 1, slot, peer, i).wait_recv()
                    copy = link(a, way, step, slot, peer, i)
                    copy.start()
                    started.append(copy)
    for way, peer, sign in streams:
        last = reach[way]
        slot = lax.rem(me + n + sign * last, n)
        for a in range(k):
            for i in range(pieces):
                link(a, way, last, slot, peer, i).wait_recv()
    for copy in started:
        copy.wait_send()
    for local in locals_:
        local.wait()


def ring_gather(arrays, n, tag, pieces=4):
    outs = tuple(jax.ShapeDtypeStruct((n,) + x.shape[1:], x.dtype) for x in arrays)
    moved = sum(x.size * x.dtype.itemsize for x in outs)
    vmem = pl.BlockSpec(memory_space=pltpu.VMEM)
    k = len(arrays)
    return pl.pallas_call(
        functools.partial(_ring_kernel, n, k, pieces),
        out_shape=outs,
        in_specs=[vmem] * k,
        out_specs=tuple([vmem] * k),
        scratch_shapes=[
            pltpu.SemaphoreType.DMA((k, 2, n // 2 + 1, pieces)),
            pltpu.SemaphoreType.DMA((k, 2, n // 2 + 1, pieces)),
            pltpu.SemaphoreType.DMA((k,)),
        ],
        compiler_params=pltpu.CompilerParams(collective_id=tag, has_side_effects=True),
        cost_estimate=pl.CostEstimate(flops=0, transcendentals=0, bytes_accessed=2 * moved),
    )(*arrays)


def per_device(
    tokens, value_weight, down_panels, up_panels, cotangent, block_adapter, adapter_slot
):
    n_owners = lax.axis_size("dp")
    myself = lax.axis_index("dp")
    n_split = lax.axis_size("mp")
    my_part = lax.axis_index("mp")
    rows, width_dev = tokens.shape
    own_rows, kv_full = cotangent.shape
    kv_part = kv_full // n_split
    stored = down_panels.shape[0]
    blocks = rows // BLOCK_ROWS
    hits = block_adapter[:, None] == jnp.arange(adapter_slot.shape[0], dtype=jnp.int32)[None, :]
    slots_all = jnp.sum(jnp.where(hits, adapter_slot[None, :], 0), axis=1)
    owner_all = (slots_all // stored).reshape(n_owners, blocks)
    local_all = (slots_all % stored).reshape(n_owners, blocks)
    mine = owner_all == myself
    wanted = jnp.sum(jnp.where(mine, local_all, 0), axis=1)
    served = jnp.any(mine, axis=1)
    pick_mask = (wanted[:, None] == jnp.arange(stored, dtype=jnp.int32)[None, :]) & served[:, None]
    my_owner = lax.dynamic_index_in_dim(owner_all, myself, 0, keepdims=False)
    select_mask = my_owner[:, None] == jnp.arange(n_owners, dtype=jnp.int32)[None, :]

    share = RANK // n_split
    up_rows_mine = lax.dynamic_slice_in_dim(up_panels, my_part * share, share, 1)
    both = jnp.concatenate([down_panels, up_rows_mine.reshape(stored, -1, RANK)], axis=1)
    got = lax.all_to_all(jnp.take(both, wanted, axis=0), "dp", split_axis=0, concat_axis=0, tiled=True)

    (cot_all,) = ring_gather([cotangent[None]], n_split, 0)
    got, cot_all = lax.optimization_barrier((got, cot_all))
    mine_got = jnp.take(got, my_owner, axis=0)
    panel_a = mine_got[:, :width_dev]
    panel_b_cols = mine_got[:, width_dev:]
    cot_all = cot_all.reshape(rows, kv_full)
    cot_blocks = cot_all.reshape(blocks, BLOCK_ROWS, kv_full)

    token_blocks = tokens.reshape(blocks, BLOCK_ROWS, width_dev)
    partial_value = jnp.dot(tokens, value_weight, preferred_element_type=jnp.float32)
    down_part = jnp.einsum(
        "bnd,bdk->bnk", token_blocks, panel_a, preferred_element_type=jnp.float32
    ).astype(jnp.bfloat16)
    down_rows = down_part.size // kv_full
    packed = jnp.concatenate(
        [down_part.reshape(down_rows, kv_full), panel_b_cols.reshape(-1, kv_full)], axis=0
    )
    (parts,) = ring_gather([packed[None]], n_split, 1, pieces=3)
    partial_value, parts = lax.optimization_barrier((partial_value, parts))
    base = lax.psum_scatter(partial_value, "mp", scatter_dimension=0, tiled=True)
    down = jnp.sum(parts[:, :down_rows].astype(jnp.float32), axis=0)
    down = down.astype(jnp.bfloat16).reshape(blocks, BLOCK_ROWS, RANK)
    parts_up = parts[:, down_rows:].reshape(n_split, blocks, share, kv_full)
    back = jnp.einsum(
        "bnc,jbqc->bnjq", cot_blocks, parts_up, preferred_element_type=jnp.float32
    ).reshape(blocks, BLOCK_ROWS, RANK).astype(jnp.bfloat16)

    first_row = my_part * own_rows
    my_down = lax.dynamic_slice_in_dim(down.reshape(rows, RANK), first_row, own_rows, 0)
    my_up = lax.dynamic_index_in_dim(parts_up, first_row // BLOCK_ROWS, 1, keepdims=False)
    my_up = my_up.reshape(RANK, kv_full)
    lifted = jnp.dot(my_down, my_up, preferred_element_type=jnp.float32)
    projected = (base + lifted).astype(jnp.bfloat16)

    select_bf = select_mask.astype(jnp.bfloat16)
    pick_bf = pick_mask.astype(jnp.bfloat16)
    down_share = lax.dynamic_slice_in_dim(down, my_part * share, share, 2)
    block_grad_b = jnp.einsum(
        "bnq,bnc->bqc", down_share, cot_blocks, preferred_element_type=jnp.float32
    )
    send_gb = jnp.einsum(
        "bo,bkc->okc", select_mask.astype(jnp.float32), block_grad_b,
        precision=lax.Precision.HIGHEST,
    )
    recv_gb = lax.all_to_all(send_gb, "dp", split_axis=0, concat_axis=0, tiled=True)
    grad_share = jnp.einsum(
        "ra,rkc->akc", pick_mask.astype(jnp.float32), recv_gb, precision=lax.Precision.HIGHEST
    ).astype(jnp.bfloat16)

    block_grad_a = jnp.einsum(
        "bnd,bnk->bdk", token_blocks, back, preferred_element_type=jnp.float32
    ).astype(jnp.bfloat16)
    send_ga = jnp.einsum(
        "bo,bdk->odk", select_bf, block_grad_a, preferred_element_type=jnp.float32
    ).astype(jnp.bfloat16)
    recv_ga = lax.all_to_all(send_ga, "dp", split_axis=0, concat_axis=0, tiled=True)
    grad_down = jnp.einsum(
        "ra,rdk->adk", pick_bf, recv_ga, preferred_element_type=jnp.float32
    ).astype(jnp.bfloat16)
    (shares,) = ring_gather([grad_share.reshape(1, -1, kv_full)], n_split, 2, pieces=2)
    shares = shares.reshape(n_split, stored, share, kv_full)
    grad_up = shares.transpose(1, 0, 2, 3).reshape(stored, RANK, kv_full)

    grad_base = jnp.einsum("nc,dc->nd", cot_all, value_weight, preferred_element_type=jnp.float32)
    through = jnp.einsum("bnk,bdk->bnd", back, panel_a, preferred_element_type=jnp.float32)
    grad_tokens = (grad_base + through.reshape(rows, width_dev)).astype(jnp.bfloat16)
    return (projected, grad_tokens, grad_down, grad_up)


def solution(mesh):
    placed = (
        P("dp", "mp"),
        P("mp", None),
        P("dp", "mp", None),
        P("dp", None, None),
        P(("dp", "mp"), None),
        P(),
        P(),
    )
    return jax.shard_map(
        per_device,
        mesh=mesh,
        in_specs=placed,
        out_specs=(P(("dp", "mp"), None), P("dp", "mp"), P("dp", "mp", None), P("dp", None, None)),
        check_vma=False,
    )
```

```python
import functools

import jax
import jax.numpy as jnp
from jax import lax
from jax.experimental import pallas as pl
from jax.experimental.pallas import tpu as pltpu
from jax.sharding import PartitionSpec as P

RANK = 64
BLOCK_ROWS = 128


def _ring_kernel(n, k, pieces, *refs):
    ins, outs = refs[:k], refs[k:2 * k]
    send_sems, recv_sems, local_sem = refs[2 * k:]
    me = lax.axis_index("mp")
    row = lax.axis_index("dp")
    right = lax.rem(me + 1, n)
    left = lax.rem(me + n - 1, n)
    barrier = pltpu.get_barrier_semaphore()
    for peer in (left, right):
        pl.semaphore_signal(
            barrier, inc=1, device_id=(row, peer), device_id_type=pl.DeviceIdType.MESH
        )
    pl.semaphore_wait(barrier, 2)
    for a in range(k):
        local = pltpu.make_async_copy(ins[a].at[0], outs[a].at[me], local_sem.at[a])
        local.start()
        local.wait()
    reach = (n // 2, n - 1 - n // 2)
    streams = ((0, right, -1), (1, left, 1))

    def link(a, way, step, slot, peer, i):
        size = outs[a].shape[1] // pieces
        part = outs[a].at[slot, pl.ds(i * size, size)]
        return pltpu.make_async_remote_copy(
            src_ref=part,
            dst_ref=part,
            send_sem=send_sems.at[a, way, step, i],
            recv_sem=recv_sems.at[a, way, step, i],
            device_id=(row, peer),
            device_id_type=pl.DeviceIdType.MESH,
        )

    started = []
    for step in range(1, reach[0] + 1):
        for way, peer, sign in streams:
            if step > reach[way]:
                continue
            slot = lax.rem(me + n + sign * (step - 1), n)
            for a in range(k):
                for i in range(pieces):
                    if step > 1:
                        link(a, way, step - 1, slot, peer, i).wait_recv()
                    copy = link(a, way, step, slot, peer, i)
                    copy.start()
                    started.append(copy)
    for way, peer, sign in streams:
        last = reach[way]
        slot = lax.rem(me + n + sign * last, n)
        for a in range(k):
            for i in range(pieces):
                link(a, way, last, slot, peer, i).wait_recv()
    for copy in started:
        copy.wait_send()


def ring_gather(arrays, n, tag, pieces=4):
    outs = tuple(jax.ShapeDtypeStruct((n,) + x.shape[1:], x.dtype) for x in arrays)
    moved = sum(x.size * x.dtype.itemsize for x in outs)
    vmem = pl.BlockSpec(memory_space=pltpu.VMEM)
    k = len(arrays)
    return pl.pallas_call(
        functools.partial(_ring_kernel, n, k, pieces),
        out_shape=outs,
        in_specs=[vmem] * k,
        out_specs=tuple([vmem] * k),
        scratch_shapes=[
            pltpu.SemaphoreType.DMA((k, 2, n // 2 + 1, pieces)),
            pltpu.SemaphoreType.DMA((k, 2, n // 2 + 1, pieces)),
            pltpu.SemaphoreType.DMA((k,)),
        ],
        compiler_params=pltpu.CompilerParams(collective_id=tag, has_side_effects=True),
        cost_estimate=pl.CostEstimate(flops=0, transcendentals=0, bytes_accessed=2 * moved),
    )(*arrays)


def per_device(
    tokens, value_weight, down_panels, up_panels, cotangent, block_adapter, adapter_slot
):
    n_owners = lax.axis_size("dp")
    myself = lax.axis_index("dp")
    n_split = lax.axis_size("mp")
    my_part = lax.axis_index("mp")
    rows, width_dev = tokens.shape
    own_rows, kv_full = cotangent.shape
    kv_part = kv_full // n_split
    stored = down_panels.shape[0]
    blocks = rows // BLOCK_ROWS
    hits = block_adapter[:, None] == jnp.arange(adapter_slot.shape[0], dtype=jnp.int32)[None, :]
    slots_all = jnp.sum(jnp.where(hits, adapter_slot[None, :], 0), axis=1)
    owner_all = (slots_all // stored).reshape(n_owners, blocks)
    local_all = (slots_all % stored).reshape(n_owners, blocks)
    mine = owner_all == myself
    wanted = jnp.sum(jnp.where(mine, local_all, 0), axis=1)
    served = jnp.any(mine, axis=1)
    pick_mask = (wanted[:, None] == jnp.arange(stored, dtype=jnp.int32)[None, :]) & served[:, None]
    my_owner = lax.dynamic_index_in_dim(owner_all, myself, 0, keepdims=False)
    select_mask = my_owner[:, None] == jnp.arange(n_owners, dtype=jnp.int32)[None, :]

    share = RANK // n_split
    up_rows_mine = lax.dynamic_slice_in_dim(up_panels, my_part * share, share, 1)
    both = jnp.concatenate([down_panels, up_rows_mine.reshape(stored, -1, RANK)], axis=1)
    got = lax.all_to_all(jnp.take(both, wanted, axis=0), "dp", split_axis=0, concat_axis=0, tiled=True)

    (cot_all,) = ring_gather([cotangent[None]], n_split, 0, pieces=2)
    got, cot_all = lax.optimization_barrier((got, cot_all))
    mine_got = jnp.take(got, my_owner, axis=0)
    panel_a = mine_got[:, :width_dev]
    panel_b_cols = mine_got[:, width_dev:]
    cot_all = cot_all.reshape(rows, kv_full)
    cot_blocks = cot_all.reshape(blocks, BLOCK_ROWS, kv_full)

    token_blocks = tokens.reshape(blocks, BLOCK_ROWS, width_dev)
    partial_value = jnp.dot(tokens, value_weight, preferred_element_type=jnp.float32)
    down_part = jnp.einsum(
        "bnd,bdk->bnk", token_blocks, panel_a, preferred_element_type=jnp.float32
    ).astype(jnp.bfloat16)
    down_rows = down_part.size // kv_full
    packed = jnp.concatenate(
        [down_part.reshape(down_rows, kv_full), panel_b_cols.reshape(-1, kv_full)], axis=0
    )
    (parts,) = ring_gather([packed[None]], n_split, 1, pieces=3)
    partial_value, parts = lax.optimization_barrier((partial_value, parts))
    base = lax.psum_scatter(partial_value, "mp", scatter_dimension=0, tiled=True)
    down = jnp.sum(parts[:, :down_rows].astype(jnp.float32), axis=0)
    down = down.astype(jnp.bfloat16).reshape(blocks, BLOCK_ROWS, RANK)
    parts_up = parts[:, down_rows:].reshape(n_split, blocks, share, kv_full)
    back = jnp.einsum(
        "bnc,jbqc->bnjq", cot_blocks, parts_up, preferred_element_type=jnp.float32
    ).reshape(blocks, BLOCK_ROWS, RANK).astype(jnp.bfloat16)

    first_row = my_part * own_rows
    my_down = lax.dynamic_slice_in_dim(down.reshape(rows, RANK), first_row, own_rows, 0)
    my_up = lax.dynamic_index_in_dim(parts_up, first_row // BLOCK_ROWS, 1, keepdims=False)
    my_up = my_up.reshape(RANK, kv_full)
    lifted = jnp.dot(my_down, my_up, preferred_element_type=jnp.float32)
    projected = (base + lifted).astype(jnp.bfloat16)

    select_bf = select_mask.astype(jnp.bfloat16)
    pick_bf = pick_mask.astype(jnp.bfloat16)
    down_share = lax.dynamic_slice_in_dim(down, my_part * share, share, 2)
    block_grad_b = jnp.einsum(
        "bnq,bnc->bqc", down_share, cot_blocks, preferred_element_type=jnp.float32
    )
    send_gb = jnp.einsum(
        "bo,bkc->okc", select_mask.astype(jnp.float32), block_grad_b,
        precision=lax.Precision.HIGHEST,
    )
    recv_gb = lax.all_to_all(send_gb, "dp", split_axis=0, concat_axis=0, tiled=True)
    grad_share = jnp.einsum(
        "ra,rkc->akc", pick_mask.astype(jnp.float32), recv_gb, precision=lax.Precision.HIGHEST
    ).astype(jnp.bfloat16)

    block_grad_a = jnp.einsum(
        "bnd,bnk->bdk", token_blocks, back, preferred_element_type=jnp.float32
    ).astype(jnp.bfloat16)
    send_ga = jnp.einsum(
        "bo,bdk->odk", select_bf, block_grad_a, preferred_element_type=jnp.float32
    ).astype(jnp.bfloat16)
    recv_ga = lax.all_to_all(send_ga, "dp", split_axis=0, concat_axis=0, tiled=True)
    grad_down = jnp.einsum(
        "ra,rdk->adk", pick_bf, recv_ga, preferred_element_type=jnp.float32
    ).astype(jnp.bfloat16)
    (shares,) = ring_gather([grad_share.reshape(1, -1, kv_full)], n_split, 2, pieces=1)
    shares = shares.reshape(n_split, stored, share, kv_full)
    grad_up = shares.transpose(1, 0, 2, 3).reshape(stored, RANK, kv_full)

    grad_base = jnp.einsum("nc,dc->nd", cot_all, value_weight, preferred_element_type=jnp.float32)
    through = jnp.einsum("bnk,bdk->bnd", back, panel_a, preferred_element_type=jnp.float32)
    grad_tokens = (grad_base + through.reshape(rows, width_dev)).astype(jnp.bfloat16)
    return (projected, grad_tokens, grad_down, grad_up)


def solution(mesh):
    placed = (
        P("dp", "mp"),
        P("mp", None),
        P("dp", "mp", None),
        P("dp", None, None),
        P(("dp", "mp"), None),
        P(),
        P(),
    )
    return jax.shard_map(
        per_device,
        mesh=mesh,
        in_specs=placed,
        out_specs=(P(("dp", "mp"), None), P("dp", "mp"), P("dp", "mp", None), P("dp", None, None)),
        check_vma=False,
    )
```

```python
import functools

import jax
import jax.numpy as jnp
from jax import lax
from jax.experimental import pallas as pl
from jax.experimental.pallas import tpu as pltpu
from jax.sharding import PartitionSpec as P

RANK = 64
BLOCK_ROWS = 128


def _ring_kernel(n, k, pieces, *refs):
    ins, outs = refs[:k], refs[k:2 * k]
    send_sems, recv_sems, local_sem = refs[2 * k:]
    me = lax.axis_index("mp")
    row = lax.axis_index("dp")
    right = lax.rem(me + 1, n)
    left = lax.rem(me + n - 1, n)
    barrier = pltpu.get_barrier_semaphore()
    for peer in (left, right):
        pl.semaphore_signal(
            barrier, inc=1, device_id=(row, peer), device_id_type=pl.DeviceIdType.MESH
        )
    pl.semaphore_wait(barrier, 2)
    for a in range(k):
        local = pltpu.make_async_copy(ins[a].at[0], outs[a].at[me], local_sem.at[a])
        local.start()
        local.wait()
    reach = (n // 2, n - 1 - n // 2)
    streams = ((0, right, -1), (1, left, 1))

    def link(a, way, step, slot, peer, i):
        size = outs[a].shape[1] // pieces
        part = outs[a].at[slot, pl.ds(i * size, size)]
        return pltpu.make_async_remote_copy(
            src_ref=part,
            dst_ref=part,
            send_sem=send_sems.at[a, way, step, i],
            recv_sem=recv_sems.at[a, way, step, i],
            device_id=(row, peer),
            device_id_type=pl.DeviceIdType.MESH,
        )

    started = []
    for step in range(1, reach[0] + 1):
        for way, peer, sign in streams:
            if step > reach[way]:
                continue
            slot = lax.rem(me + n + sign * (step - 1), n)
            for a in range(k):
                for i in range(pieces):
                    if step > 1:
                        link(a, way, step - 1, slot, peer, i).wait_recv()
                    copy = link(a, way, step, slot, peer, i)
                    copy.start()
                    started.append(copy)
    for way, peer, sign in streams:
        last = reach[way]
        slot = lax.rem(me + n + sign * last, n)
        for a in range(k):
            for i in range(pieces):
                link(a, way, last, slot, peer, i).wait_recv()
    for copy in started:
        copy.wait_send()


def ring_gather(arrays, n, tag, pieces=4):
    outs = tuple(jax.ShapeDtypeStruct((n,) + x.shape[1:], x.dtype) for x in arrays)
    moved = sum(x.size * x.dtype.itemsize for x in outs)
    vmem = pl.BlockSpec(memory_space=pltpu.VMEM)
    k = len(arrays)
    return pl.pallas_call(
        functools.partial(_ring_kernel, n, k, pieces),
        out_shape=outs,
        in_specs=[vmem] * k,
        out_specs=tuple([vmem] * k),
        scratch_shapes=[
            pltpu.SemaphoreType.DMA((k, 2, n // 2 + 1, pieces)),
            pltpu.SemaphoreType.DMA((k, 2, n // 2 + 1, pieces)),
            pltpu.SemaphoreType.DMA((k,)),
        ],
        compiler_params=pltpu.CompilerParams(collective_id=tag, has_side_effects=True),
        cost_estimate=pl.CostEstimate(flops=0, transcendentals=0, bytes_accessed=2 * moved),
    )(*arrays)


def per_device(
    tokens, value_weight, down_panels, up_panels, cotangent, block_adapter, adapter_slot
):
    n_owners = lax.axis_size("dp")
    myself = lax.axis_index("dp")
    n_split = lax.axis_size("mp")
    my_part = lax.axis_index("mp")
    rows, width_dev = tokens.shape
    own_rows, kv_full = cotangent.shape
    kv_part = kv_full // n_split
    stored = down_panels.shape[0]
    blocks = rows // BLOCK_ROWS
    hits = block_adapter[:, None] == jnp.arange(adapter_slot.shape[0], dtype=jnp.int32)[None, :]
    slots_all = jnp.sum(jnp.where(hits, adapter_slot[None, :], 0), axis=1)
    owner_all = (slots_all // stored).reshape(n_owners, blocks)
    local_all = (slots_all % stored).reshape(n_owners, blocks)
    mine = owner_all == myself
    wanted = jnp.sum(jnp.where(mine, local_all, 0), axis=1)
    served = jnp.any(mine, axis=1)
    pick_mask = (wanted[:, None] == jnp.arange(stored, dtype=jnp.int32)[None, :]) & served[:, None]
    my_owner = lax.dynamic_index_in_dim(owner_all, myself, 0, keepdims=False)
    select_mask = my_owner[:, None] == jnp.arange(n_owners, dtype=jnp.int32)[None, :]

    share = RANK // n_split
    up_rows_mine = lax.dynamic_slice_in_dim(up_panels, my_part * share, share, 1)
    both = jnp.concatenate([down_panels, up_rows_mine.reshape(stored, -1, RANK)], axis=1)
    got = lax.all_to_all(jnp.take(both, wanted, axis=0), "dp", split_axis=0, concat_axis=0, tiled=True)

    (cot_all,) = ring_gather([cotangent[None]], n_split, 0)
    got, cot_all = lax.optimization_barrier((got, cot_all))
    mine_got = jnp.take(got, my_owner, axis=0)
    panel_a = mine_got[:, :width_dev]
    panel_b_cols = mine_got[:, width_dev:]
    cot_all = cot_all.reshape(rows, kv_full)
    cot_blocks = cot_all.reshape(blocks, BLOCK_ROWS, kv_full)

    token_blocks = tokens.reshape(blocks, BLOCK_ROWS, width_dev)
    partial_value = jnp.dot(tokens, value_weight, preferred_element_type=jnp.float32)
    down_part = jnp.einsum(
        "bnd,bdk->bnk", token_blocks, panel_a, preferred_element_type=jnp.float32
    ).astype(jnp.bfloat16)
    down_rows = down_part.size // kv_full
    packed = jnp.concatenate(
        [down_part.reshape(down_rows, kv_full), panel_b_cols.reshape(-1, kv_full)], axis=0
    )
    (parts,) = ring_gather([packed[None]], n_split, 1, pieces=2)
    partial_value, parts = lax.optimization_barrier((partial_value, parts))
    base = lax.psum_scatter(partial_value, "mp", scatter_dimension=0, tiled=True)
    down = jnp.sum(parts[:, :down_rows].astype(jnp.float32), axis=0)
    down = down.astype(jnp.bfloat16).reshape(blocks, BLOCK_ROWS, RANK)
    parts_up = parts[:, down_rows:].reshape(n_split, blocks, share, kv_full)
    back = jnp.einsum(
        "bnc,jbqc->bnjq", cot_blocks, parts_up, preferred_element_type=jnp.float32
    ).reshape(blocks, BLOCK_ROWS, RANK).astype(jnp.bfloat16)

    first_row = my_part * own_rows
    my_down = lax.dynamic_slice_in_dim(down.reshape(rows, RANK), first_row, own_rows, 0)
    my_up = lax.dynamic_index_in_dim(parts_up, first_row // BLOCK_ROWS, 1, keepdims=False)
    my_up = my_up.reshape(RANK, kv_full)
    lifted = jnp.dot(my_down, my_up, preferred_element_type=jnp.float32)
    projected = (base + lifted).astype(jnp.bfloat16)

    select_bf = select_mask.astype(jnp.bfloat16)
    pick_bf = pick_mask.astype(jnp.bfloat16)
    down_share = lax.dynamic_slice_in_dim(down, my_part * share, share, 2)
    block_grad_b = jnp.einsum(
        "bnq,bnc->bqc", down_share, cot_blocks, preferred_element_type=jnp.float32
    )
    send_gb = jnp.einsum(
        "bo,bkc->okc", select_mask.astype(jnp.float32), block_grad_b,
        precision=lax.Precision.HIGHEST,
    )
    recv_gb = lax.all_to_all(send_gb, "dp", split_axis=0, concat_axis=0, tiled=True)
    grad_share = jnp.einsum(
        "ra,rkc->akc", pick_mask.astype(jnp.float32), recv_gb, precision=lax.Precision.HIGHEST
    ).astype(jnp.bfloat16)

    block_grad_a = jnp.einsum(
        "bnd,bnk->bdk", token_blocks, back, preferred_element_type=jnp.float32
    ).astype(jnp.bfloat16)
    send_ga = jnp.einsum(
        "bo,bdk->odk", select_bf, block_grad_a, preferred_element_type=jnp.float32
    ).astype(jnp.bfloat16)
    recv_ga = lax.all_to_all(send_ga, "dp", split_axis=0, concat_axis=0, tiled=True)
    grad_down = jnp.einsum(
        "ra,rdk->adk", pick_bf, recv_ga, preferred_element_type=jnp.float32
    ).astype(jnp.bfloat16)
    (shares,) = ring_gather([grad_share.reshape(1, -1, kv_full)], n_split, 2, pieces=2)
    shares = shares.reshape(n_split, stored, share, kv_full)
    grad_up = shares.transpose(1, 0, 2, 3).reshape(stored, RANK, kv_full)

    grad_base = jnp.einsum("nc,dc->nd", cot_all, value_weight, preferred_element_type=jnp.float32)
    through = jnp.einsum("bnk,bdk->bnd", back, panel_a, preferred_element_type=jnp.float32)
    grad_tokens = (grad_base + through.reshape(rows, width_dev)).astype(jnp.bfloat16)
    return (projected, grad_tokens, grad_down, grad_up)


def solution(mesh):
    placed = (
        P("dp", "mp"),
        P("mp", None),
        P("dp", "mp", None),
        P("dp", None, None),
        P(("dp", "mp"), None),
        P(),
        P(),
    )
    return jax.shard_map(
        per_device,
        mesh=mesh,
        in_specs=placed,
        out_specs=(P(("dp", "mp"), None), P("dp", "mp"), P("dp", "mp", None), P("dp", None, None)),
        check_vma=False,
    )
```
